32 devices in a mesh: group: 2 (over x), strip: 16 (over z, y, core).
Axes of the slice: x: 2, y: 2, z: 4, core: 2. Of those that a mesh axis runs over, the one named last changes fastest.
Arguments:
- frame_tokens: bfloat16 [16384, 768], P(('group', 'strip')), parts along dimension 0, may hold values from -6 to 6
- window_reach: int32 [32], P('group'), parts along dimension 0, may hold values from 64 to 128, as said below
- valid_count: int32 [32], P('group'), parts along dimension 0, may hold values from 256 to 512, as said below
- space_gain: float32 [768], replicated, may hold values from 0.1 to 1.9
- space_project: bfloat16 [768, 2304], replicated, may hold values from -32 to 32
- space_output: bfloat16 [768, 768], replicated, may hold values from -0.21875 to 0.21875
- time_gain: float32 [768], replicated, may hold values from 0.1 to 1.9
- time_project: bfloat16 [768, 2304], replicated, may hold values from -32 to 32
- time_output: bfloat16 [768, 768], replicated, may hold values from -0.21875 to 0.21875
Outputs:
- restored: bfloat16 [16384, 768], P(('group', 'strip')), parts along dimension 0
The draws below stay inside these ranges and needn't reach their ends.
There are 2 independent parts, one for each index of `group`. The reference program is written for one: setup_inputs(seed, part) draws one part's arguments, and reference() takes and returns one part's arrays. A program takes and returns all parts, laid end to end along the dimension named above; an argument that names none is the same for every part. Nothing has to cross between parts.
Inputs may be any that keep to these rules, and one draw needn't show every extreme that they name: `window_reach`: some frame has reach exactly 128. `valid_count`: some frame is fully valid.
All inputs are finite; a program needn't handle non-finite values.
Results may differ from the reference program's by a relative error of at most 0.01.
Values may be sent and summed in bfloat16 or wider, within the bound.
No kernel may reach another device: no remote copies, remote signals or barrier semaphores. Data moves between devices by JAX's collectives and lax.ppermute only.
A program may use at most 128 MiB of HBM per device.

```python
import jax
import jax.numpy as jnp
from jax import lax

TOK_DEV = 512
F = 16
HALO = 128
LAYERS = 2
H = 12
HD = 64
D = 768
FRAME_TOK = 512
TOKENS = 8192


def clipped_weight(key):
    base = jnp.clip(jax.random.normal(key, (D, 3 * D), jnp.float32), -6.0, 6.0) * D ** (-0.5)
    return base.astype(jnp.bfloat16)


def draw_space_project(key, part):
    return clipped_weight(jax.random.fold_in(key, 11))


def draw_time_project(key, part):
    return clipped_weight(jax.random.fold_in(key, 12))


def with_largest(key, lowest, highest):
    values = jax.random.randint(key, (F,), lowest, highest + 1, jnp.int32)
    chosen = jax.random.randint(jax.random.fold_in(key, 3), (), 0, F, jnp.int32)
    return jnp.where(jnp.arange(F, dtype=jnp.int32) == chosen, highest, values).astype(jnp.int32)


def draw_window_reach(key, part):
    return with_largest(jax.random.fold_in(key, 21), HALO // 2, HALO)


def draw_valid_count(key, part):
    return with_largest(jax.random.fold_in(key, 22), FRAME_TOK // 2, FRAME_TOK)


def steps_of(own_key, dims, cuts, low, high):
    level, own = 1.0, jax.random.fold_in(own_key, 6)
    for dim, parts in cuts:
        draws = jnp.exp(jax.random.uniform(jax.random.fold_in(own, dim), (parts,), jnp.float32, low / len(cuts), high / len(cuts)))
        level = level * jnp.repeat(draws, dims[dim] // parts).reshape([-1 if axis == dim else 1 for axis in range(len(dims))])
    return level


def gaussian(stream_key, shape, spread, limit, pieces=(), kind=jnp.bfloat16):
    factor_of = steps_of(stream_key, shape, pieces, -0.22, 0.18) if pieces else 1.0
    values = jax.random.normal(stream_key, shape, jnp.float32) * spread * factor_of
    return jnp.minimum(jnp.maximum(values, -limit), limit).astype(kind)


def setup_inputs(seed: int = 0, part: int = 0) -> dict:
    key_of = jax.random.split(jax.random.key(seed), 10)
    part_keys = jax.random.split(jax.random.fold_in(key_of[9], part), 10)
    return {
        "frame_tokens": gaussian(part_keys[0], (TOKENS, D), 1.0, 6.0, ((0, 16),)),
        "window_reach": draw_window_reach(jax.random.fold_in(jax.random.fold_in(key_of[9], part), 71), part),
        "valid_count": draw_valid_count(jax.random.fold_in(jax.random.fold_in(key_of[9], part), 71), part),
        "space_gain": jnp.clip(1.0 + 0.18 * jax.random.normal(key_of[3], (D,), jnp.float32), 0.1, 1.9),
        "space_project": draw_space_project(jax.random.fold_in(key_of[9], 71), part),
        "space_output": gaussian(key_of[5], (D, D), D ** -0.5, 0.21875),
        "time_gain": jnp.clip(1.0 + 0.18 * jax.random.normal(key_of[6], (D,), jnp.float32), 0.1, 1.9),
        "time_project": draw_time_project(jax.random.fold_in(key_of[9], 71), part),
        "time_output": gaussian(key_of[8], (D, D), D ** -0.5, 0.21875),
    }


epsilon = 1e-06

def normed(values, gain):
    wide = values.astype(jnp.float32)
    meansq = lax.optimization_barrier(jnp.mean(wide * wide, axis=-1, keepdims=True))
    return (wide * lax.rsqrt(meansq + epsilon) * gain).astype(jnp.bfloat16)

def lookup(table, index):
    hits = index[:, None] == jnp.arange(table.shape[0], dtype=jnp.int32)[None, :]
    return lax.optimization_barrier(jnp.sum(jnp.where(hits, table[None, :], 0), axis=-1)).astype(jnp.int32)

def make_mask(query_pos, key_pos, window_reach, valid_count, frame_len, total):
    distance = jnp.abs(query_pos[:, None] - key_pos[None, :])
    inside = (key_pos >= 0) & (key_pos < total)
    clamped = jnp.clip(key_pos, 0, total - 1).astype(jnp.int32)
    key_count = lookup(valid_count, (clamped // frame_len).astype(jnp.int32))
    reach_rows = lookup(window_reach, (query_pos // frame_len).astype(jnp.int32))
    living = (clamped % frame_len >= frame_len - key_count)[None, :] | (distance == 0)
    return (distance <= reach_rows[:, None]) & inside[None, :] & living

def attend(query_rows, key_rows, value_rows, allowed):
    rows_q = query_rows.shape[0]
    rows_k = key_rows.shape[0]
    query_heads = query_rows.astype(jnp.float32).reshape(rows_q, H, HD)
    key_heads = key_rows.astype(jnp.float32).reshape(rows_k, H, HD)
    value_heads = value_rows.astype(jnp.float32).reshape(rows_k, H, HD)
    scores = jnp.einsum('qhd,khd->hqk', query_heads, key_heads) * HD ** (-0.5)
    scores = jnp.where(allowed[None], scores, -jnp.inf)
    highest = lax.optimization_barrier(jnp.max(scores, axis=-1, keepdims=True))
    expon = jnp.exp(scores - highest)
    weights = (expon / lax.optimization_barrier(jnp.sum(expon, axis=-1, keepdims=True))).astype(jnp.bfloat16)
    mixed = jnp.einsum('hqk,khd->qhd', weights.astype(jnp.float32), value_heads)
    return mixed.astype(jnp.bfloat16).reshape(rows_q, H * HD)

def temporal(columns, positions, valid_count):
    count = columns.shape[1]
    wide = columns.astype(jnp.float32).reshape(F, count, 3, H, HD)
    scores = jnp.einsum('fphd,gphd->hpfg', wide[:, :, 0], wide[:, :, 1]) * HD ** (-0.5)
    living = positions[:, None] >= FRAME_TOK - valid_count[None, :]
    diagonal = jnp.eye(F, dtype=bool)
    allowed = living[:, None, :] | diagonal[None]
    scores = jnp.where(allowed[None], scores, -jnp.inf)
    highest = lax.optimization_barrier(jnp.max(scores, axis=-1, keepdims=True))
    expon = jnp.exp(scores - highest)
    weights = (expon / lax.optimization_barrier(jnp.sum(expon, axis=-1, keepdims=True))).astype(jnp.bfloat16)
    mixed = jnp.einsum('hpfg,gphd->fphd', weights.astype(jnp.float32), wide[:, :, 2])
    return mixed.astype(jnp.bfloat16).reshape(F, count, H * HD)

def space_layer(state, gain, project, output, window_reach, valid_count):
    hidden = normed(state, gain)
    projected = jnp.dot(hidden, project, preferred_element_type=jnp.float32).astype(jnp.bfloat16)
    padded = jnp.pad(projected, ((HALO, HALO), (0, 0)))
    blocks = TOKENS // TOK_DEV

    def one_block(index):
        start = (index * TOK_DEV).astype(jnp.int32)
        query_rows = lax.dynamic_slice(projected, (start, jnp.int32(0)), (TOK_DEV, D))
        beside_all = lax.dynamic_slice(padded, (start, jnp.int32(D)), (TOK_DEV + 2 * HALO, 2 * D))
        query_pos = start + jnp.arange(TOK_DEV, dtype=jnp.int32)
        key_pos = start - HALO + jnp.arange(TOK_DEV + 2 * HALO, dtype=jnp.int32)
        allowed = make_mask(query_pos, key_pos, window_reach, valid_count, FRAME_TOK, TOKENS)
        return attend(query_rows, beside_all[:, :D], beside_all[:, D:], allowed)
    mixed = lax.map(one_block, jnp.arange(blocks, dtype=jnp.int32)).reshape(TOKENS, D)
    update = jnp.dot(mixed, output, preferred_element_type=jnp.float32)
    return (state.astype(jnp.float32) + update).astype(jnp.bfloat16)

def reference(frame_tokens, window_reach, valid_count, space_gain, space_project, space_output, time_gain, time_project, time_output):
    state = frame_tokens
    for layer in range(LAYERS):
        state = space_layer(state, space_gain, space_project, space_output, window_reach, valid_count)
    hidden = normed(state, time_gain)
    projected = jnp.dot(hidden, time_project, preferred_element_type=jnp.float32).astype(jnp.bfloat16)
    positions = jnp.arange(FRAME_TOK, dtype=jnp.int32)
    mixed = temporal(projected.reshape(F, FRAME_TOK, 3 * D), positions, valid_count)
    update = jnp.dot(mixed.reshape(F * FRAME_TOK, D), time_output, preferred_element_type=jnp.float32).astype(jnp.bfloat16)
    return (state.astype(jnp.float32) + update.astype(jnp.float32)).astype(jnp.bfloat16)
```

```python
import functools

import jax
import jax.numpy as jnp
from jax import lax
from jax.experimental import pallas as pl
from jax.experimental.pallas import tpu as pltpu
from jax.sharding import PartitionSpec as P

F = 16
HALO = 128
H = 12
HD = 64
D = 768
BLK = HALO
WIN = 3 * BLK
PAIR = 2 * HD
CHUNK = 2 * BLK
COLS = 256
EPS = 1e-06
MASKED = -1e30

BF16 = jnp.bfloat16
F32 = jnp.float32


def norm_rows(values, gain):
    wide = values.astype(F32)
    meansq = jnp.mean(wide * wide, axis=-1, keepdims=True)
    return (wide * lax.rsqrt(meansq + EPS) * gain).astype(BF16)


def project(x, weight_ref, first, last, store):
    def step(i, carry):
        at = pl.multiple_of(first + i * COLS, COLS)
        store(at, jnp.dot(x, weight_ref[:, pl.ds(at, COLS)], preferred_element_type=F32))
        return carry

    lax.fori_loop(0, (last - first) // COLS, step, 0)


def pair_attention(q, k, v, bias):
    rows = q.shape[0]
    lane = lax.broadcasted_iota(jnp.int32, (1, PAIR), 1)
    scale = HD ** (-0.5)
    left = jnp.where(lane < HD, scale, 0.0).astype(BF16)
    right = jnp.where(lane < HD, 0.0, scale).astype(BF16)
    both = jnp.concatenate([q * left, q * right], axis=0)
    scores = lax.dot_general(both, k, (((1,), (1,)), ((), ())), preferred_element_type=F32)
    scores = scores.reshape(2, rows, -1) + bias[None]
    highest = jnp.max(scores, axis=-1, keepdims=True)
    expon = jnp.exp(scores - highest)
    total = jnp.sum(expon, axis=-1, keepdims=True)
    mixed = jnp.dot(expon.reshape(2 * rows, -1).astype(BF16), v, preferred_element_type=F32)
    mixed = mixed.reshape(2, rows, PAIR) * (1.0 / total)
    return jnp.where(lane < HD, mixed[0], mixed[1]).astype(BF16)


def window_bias(start, reach_ref, count_ref, frame_len, total):
    row = lax.broadcasted_iota(jnp.int32, (BLK, WIN), 0)
    col = lax.broadcasted_iota(jnp.int32, (BLK, WIN), 1)
    distance = col - BLK - row
    reach = reach_ref[lax.div(jnp.clip(start, 0, total - 1), frame_len)]
    least = jnp.zeros((1, WIN), jnp.int32)
    place = lax.broadcasted_iota(jnp.int32, (1, WIN), 1)
    for j in range(3):
        at = start + (j - 1) * BLK
        inside = (at >= 0) & (at < total)
        frame = lax.div(jnp.clip(at, 0, total - 1), frame_len)
        first = (frame + 1) * frame_len - count_ref[frame] - at
        first = jnp.where(inside, first, WIN) + j * BLK
        least = jnp.where(place >= j * BLK, first, least)
    living = (col >= least) | (distance == 0)
    return jnp.where((jnp.abs(distance) <= reach) & living, 0.0, MASKED).astype(F32)


def space_attention(blocks, start_of, q_ref, k_ref, v_ref, bias_ref, mixed_ref, tables):
    def one_block(i, carry):
        rows = pl.ds(pl.multiple_of(i * BLK, BLK), BLK)
        keys = pl.ds(pl.multiple_of(i * BLK, BLK), WIN)
        bias_ref[...] = window_bias(start_of(i), *tables)
        for pair in range(H // 2):
            lanes = slice(pair * PAIR, (pair + 1) * PAIR)
            mixed_ref[rows, lanes] = pair_attention(
                q_ref[rows, lanes], k_ref[keys, lanes], v_ref[keys, lanes], bias_ref[...]
            )
        return carry

    lax.fori_loop(0, blocks, one_block, 0)


def middle_kernel(
    frame_len,
    total,
    reach_ref,
    count_ref,
    index_ref,
    x_ref,
    gain_ref,
    project_ref,
    output_ref,
    first_ref,
    state_ref,
    second_ref,
    q_s,
    k_s,
    v_s,
    mixed_s,
    bias_s,
):
    rows = x_ref.shape[0]
    inner = rows - 2 * BLK
    offset = index_ref[0] * rows
    gain = gain_ref[...]

    def store_first(at, value):
        first_ref[:, pl.ds(at, COLS)] = value.astype(BF16)

    project(norm_rows(x_ref[...], gain), project_ref, 0, 3 * D, store_first)
    q_s[...] = first_ref[BLK : rows - BLK, :D]
    k_s[...] = first_ref[:, D : 2 * D]
    v_s[...] = first_ref[:, 2 * D :]
    tables = (reach_ref, count_ref, frame_len, total)
    space_attention(
        inner // BLK, lambda i: offset + (i + 1) * BLK, q_s, k_s, v_s, bias_s, mixed_s, tables
    )

    def store_state(at, value):
        old = x_ref[BLK : rows - BLK, pl.ds(at, COLS)].astype(F32)
        state_ref[:, pl.ds(at, COLS)] = (old + value).astype(BF16)

    project(mixed_s[...], output_ref, 0, D, store_state)

    def store_second(at, value):
        second_ref[:, pl.ds(at, COLS)] = value.astype(BF16)

    project(norm_rows(state_ref[...], gain), project_ref, 0, 3 * D, store_second)


def side_kernel(
    frame_len,
    total,
    local_rows,
    after,
    reach_ref,
    count_ref,
    index_ref,
    halo_ref,
    x_ref,
    first_ref,
    middle_ref,
    second_ref,
    gain_ref,
    time_gain_ref,
    project_ref,
    output_ref,
    state_ref,
    hidden_ref,
    q_s,
    k_s,
    v_s,
    mixed_s,
    edge_s,
    bias_s,
):
    offset = index_ref[0] * local_rows
    gain = gain_ref[...]
    half = 2 * BLK
    tables = (reach_ref, count_ref, frame_len, total)
    if after:
        start = offset + local_rows - half
        own, far = 0, half
        own_edge = slice(half - BLK, half)
        far_edge = slice(0, BLK)
        edge_blocks = (0, BLK)
    else:
        start = offset - half
        own, far = half, 0
        own_edge = slice(0, BLK)
        far_edge = slice(BLK, half)
        edge_blocks = (BLK, 0)
    own_at, far_at = edge_blocks
    k_s[own : own + half, :] = first_ref[:, D : 2 * D]
    v_s[own : own + half, :] = first_ref[:, 2 * D :]
    q_s[own_at : own_at + BLK, :] = first_ref[own_edge, :D]
    hidden = norm_rows(halo_ref[...], gain)

    def store_query(at, value):
        q_s[far_at : far_at + BLK, pl.ds(at, COLS)] = value.astype(BF16)

    def store_key(at, value):
        k_s[far : far + half, pl.ds(at - D, COLS)] = value.astype(BF16)

    def store_value(at, value):
        v_s[far : far + half, pl.ds(at - 2 * D, COLS)] = value.astype(BF16)

    project(hidden[far_edge], project_ref, 0, D, store_query)
    project(hidden, project_ref, D, 2 * D, store_key)
    project(hidden, project_ref, 2 * D, 3 * D, store_value)
    space_attention(2, lambda i: start + (i + 1) * BLK, q_s, k_s, v_s, bias_s, mixed_s, tables)

    def store_edge(at, value):
        cols = pl.ds(at, COLS)
        edge_s[own_at : own_at + BLK, cols] = (
            x_ref[own_edge, cols].astype(F32) + value[own_at : own_at + BLK]
        ).astype(BF16)
        edge_s[far_at : far_at + BLK, cols] = (
            halo_ref[far_edge, cols].astype(F32) + value[far_at : far_at + BLK]
        ).astype(BF16)

    project(mixed_s[...], output_ref, 0, D, store_edge)

    if after:
        mid, edge, begin = 0, half, start - BLK
        own_mid = slice(BLK, half)
        q_mid, q_edge = 0, BLK
    else:
        mid, edge, begin = half, 0, start + BLK
        own_mid = slice(0, BLK)
        q_mid, q_edge = BLK, 0
    k_s[mid : mid + half, :] = second_ref[:, D : 2 * D]
    v_s[mid : mid + half, :] = second_ref[:, 2 * D :]
    q_s[q_mid : q_mid + BLK, :] = second_ref[own_mid, :D]
    hidden = norm_rows(edge_s[...], gain)

    def store_query2(at, value):
        q_s[q_edge : q_edge + BLK, pl.ds(at, COLS)] = value.astype(BF16)

    def store_key2(at, value):
        k_s[edge : edge + half, pl.ds(at - D, COLS)] = value.astype(BF16)

    def store_value2(at, value):
        v_s[edge : edge + half, pl.ds(at - 2 * D, COLS)] = value.astype(BF16)

    project(hidden[own_at : own_at + BLK], project_ref, 0, D, store_query2)
    project(hidden, project_ref, D, 2 * D, store_key2)
    project(hidden, project_ref, 2 * D, 3 * D, store_value2)
    space_attention(2, lambda i: begin + (i + 1) * BLK, q_s, k_s, v_s, bias_s, mixed_s, tables)

    def store_state(at, value):
        cols = pl.ds(at, COLS)
        state_ref[q_edge : q_edge + BLK, cols] = (
            edge_s[own_at : own_at + BLK, cols].astype(F32) + value[q_edge : q_edge + BLK]
        ).astype(BF16)
        state_ref[q_mid : q_mid + BLK, cols] = (
            middle_ref[own_mid, cols].astype(F32) + value[q_mid : q_mid + BLK]
        ).astype(BF16)

    project(mixed_s[...], output_ref, 0, D, store_state)
    hidden_ref[...] = norm_rows(state_ref[...], time_gain_ref[...])


def time_kernel(
    frame_len,
    local_rows,
    devices,
    chunk,
    count_ref,
    index_ref,
    x_ref,
    project_ref,
    output_ref,
    update_ref,
    qkv_s,
    mixed_s,
    bias_s,
):
    rows = x_ref.shape[0]
    slots = rows // F
    piece = rows // devices

    def store_qkv(at, value):
        qkv_s[:, pl.ds(at, COLS)] = value.astype(BF16)

    project(x_ref[...], project_ref, 0, 3 * D, store_qkv)
    row = lax.broadcasted_iota(jnp.int32, (rows, rows), 0)
    col = lax.broadcasted_iota(jnp.int32, (rows, rows), 1)
    key = lax.broadcasted_iota(jnp.int32, (1, rows), 1)
    key_frame = lax.div(key, slots)
    key_slot = lax.rem(key, slots)
    place = lax.div(key_slot, piece) * local_rows + lax.rem(key_slot, piece)
    place = place + chunk * rows + index_ref[0] * piece
    least = jnp.zeros((1, rows), jnp.int32)
    for g in range(F):
        least = jnp.where(key_frame == g, frame_len - count_ref[g], least)
    living = jnp.where(place >= least, 1, 0)
    same = lax.rem(row, slots) == lax.rem(col, slots)
    bias_s[...] = jnp.where(same & ((living == 1) | (row == col)), 0.0, MASKED).astype(F32)

    for pair in range(H // 2):
        lanes = slice(pair * PAIR, (pair + 1) * PAIR)
        mixed_s[:, lanes] = pair_attention(
            qkv_s[:, lanes],
            qkv_s[:, D + pair * PAIR : D + (pair + 1) * PAIR],
            qkv_s[:, 2 * D + pair * PAIR : 2 * D + (pair + 1) * PAIR],
            bias_s[...],
        )

    def store_update(at, value):
        update_ref[:, pl.ds(at, COLS)] = value.astype(BF16)

    project(mixed_s[...], output_ref, 0, D, store_update)


def smem():
    return pl.BlockSpec(memory_space=pltpu.SMEM)


def rows_of(block_rows, cols, at):
    return pl.BlockSpec((block_rows, cols), lambda i: (at, 0))


def whole(shape):
    return pl.BlockSpec(shape, lambda i: (0,) * len(shape))


def params():
    return pltpu.CompilerParams(
        dimension_semantics=("arbitrary",), vmem_limit_bytes=32 << 20
    )


def cost(flops, bytes_accessed, exps):
    return pl.CostEstimate(flops=flops, bytes_accessed=bytes_accessed, transcendentals=exps)


def on_device(
    frame_tokens,
    window_reach,
    valid_count,
    space_gain,
    space_project,
    space_output,
    time_gain,
    time_project,
    time_output,
):
    devices = lax.axis_size("strip")
    local_rows = frame_tokens.shape[0]
    total = local_rows * devices
    frame_len = total // F
    if local_rows != 2 * CHUNK or frame_len % local_rows or CHUNK % devices:
        raise ValueError("unsupported sizes")
    index = lax.axis_index("strip").reshape(1)
    gain = space_gain.reshape(1, D)
    gain_t = time_gain.reshape(1, D)

    up = [(i, i + 1) for i in range(devices - 1)]
    down = [(i + 1, i) for i in range(devices - 1)]
    before = lax.ppermute(frame_tokens[local_rows - CHUNK :], "strip", up)
    after = lax.ppermute(frame_tokens[:CHUNK], "strip", down)

    weight_bytes = 2 * D * 4 * D
    first, middle, second = pl.pallas_call(
        functools.partial(middle_kernel, frame_len, total),
        grid=(1,),
        out_shape=(
            jax.ShapeDtypeStruct((local_rows, 3 * D), BF16),
            jax.ShapeDtypeStruct((CHUNK, D), BF16),
            jax.ShapeDtypeStruct((CHUNK, 3 * D), BF16),
        ),
        in_specs=[smem(), smem(), smem(), whole((local_rows, D)), whole((1, D)), whole((D, 3 * D)), whole((D, D))],
        out_specs=(whole((local_rows, 3 * D)), whole((CHUNK, D)), whole((CHUNK, 3 * D))),
        scratch_shapes=[
            pltpu.VMEM((CHUNK, D), BF16),
            pltpu.VMEM((local_rows, D), BF16),
            pltpu.VMEM((local_rows, D), BF16),
            pltpu.VMEM((CHUNK, D), BF16),
            pltpu.VMEM((BLK, WIN), F32),
        ],
        compiler_params=params(),
        cost_estimate=cost(2 * D * D * 3 * 3 * CHUNK, weight_bytes, H * CHUNK * WIN),
        name="middle",
    )(window_reach, valid_count, index, frame_tokens, gain, space_project, space_output)

    def side(halo, is_after):
        at = 1 if is_after else 0
        return pl.pallas_call(
            functools.partial(side_kernel, frame_len, total, local_rows, is_after),
            grid=(1,),
            out_shape=(jax.ShapeDtypeStruct((CHUNK, D), BF16),) * 2,
            in_specs=[
                smem(),
                smem(),
                smem(),
                whole((CHUNK, D)),
                rows_of(CHUNK, D, at),
                rows_of(CHUNK, 3 * D, at),
                whole((CHUNK, D)),
                whole((CHUNK, 3 * D)),
                whole((1, D)),
                whole((1, D)),
                whole((D, 3 * D)),
                whole((D, D)),
            ],
            out_specs=(whole((CHUNK, D)),) * 2,
            scratch_shapes=[
                pltpu.VMEM((CHUNK, D), BF16),
                pltpu.VMEM((2 * CHUNK, D), BF16),
                pltpu.VMEM((2 * CHUNK, D), BF16),
                pltpu.VMEM((CHUNK, D), BF16),
                pltpu.VMEM((CHUNK, D), BF16),
                pltpu.VMEM((BLK, WIN), F32),
            ],
            compiler_params=params(),
            cost_estimate=cost(2 * D * D * 8 * CHUNK, weight_bytes, 2 * H * CHUNK * WIN),
            name="after" if is_after else "before",
        )(
            window_reach,
            valid_count,
            index,
            halo,
            frame_tokens,
            first,
            middle,
            second,
            gain,
            gain_t,
            space_project,
            space_output,
        )

    def exchange(x):
        return lax.all_to_all(x, "strip", split_axis=0, concat_axis=0, tiled=True)

    def temporal(x, chunk):
        return pl.pallas_call(
            functools.partial(time_kernel, frame_len, local_rows, devices, chunk),
            grid=(1,),
            out_shape=jax.ShapeDtypeStruct((CHUNK, D), BF16),
            in_specs=[smem(), smem(), whole((CHUNK, D)), whole((D, 3 * D)), whole((D, D))],
            out_specs=whole((CHUNK, D)),
            scratch_shapes=[
                pltpu.VMEM((CHUNK, 3 * D), BF16),
                pltpu.VMEM((CHUNK, D), BF16),
                pltpu.VMEM((CHUNK, CHUNK), F32),
            ],
            compiler_params=params(),
            cost_estimate=cost(2 * D * D * 5 * CHUNK, weight_bytes, H * CHUNK * CHUNK),
            name="time%d" % chunk,
        )(valid_count, index, x, time_project, time_output)

    state0, hidden0 = side(before, False)
    sent0 = exchange(hidden0)
    state1, hidden1 = side(after, True)
    sent1 = exchange(hidden1)
    back0 = exchange(temporal(sent0, 0))
    back1 = exchange(temporal(sent1, 1))
    wide = [
        (s.astype(F32) + b.astype(F32)).astype(BF16) for s, b in ((state0, back0), (state1, back1))
    ]
    return jnp.concatenate(wide, axis=0)


def solution(mesh):
    return jax.shard_map(
        on_device,
        mesh=mesh,
        in_specs=(
            P(("group", "strip"), None),
            P("group"),
            P("group"),
            P(),
            P(),
            P(),
            P(),
            P(),
            P(),
        ),
        out_specs=P(("group", "strip"), None),
        check_vma=False,
    )
```

```python
import functools

import jax
import jax.numpy as jnp
from jax import lax
from jax.experimental import pallas as pl
from jax.experimental.pallas import tpu as pltpu
from jax.sharding import PartitionSpec as P


F = 16
HALO = 128
H = 12
HD = 64
D = 768
BLK = HALO
WIN = 3 * BLK
PAIR = 2 * HD
CHUNK = 2 * BLK
VMEM_LIMIT = 60 * 1024 * 1024
EPS = 1e-06
MASKED = -1e30

BF16 = jnp.bfloat16
F32 = jnp.float32


def norm_rows(values, gain):
    wide = values.astype(F32)
    meansq = jnp.mean(wide * wide, axis=-1, keepdims=True)
    return (wide * lax.rsqrt(meansq + EPS) * gain).astype(BF16)


def pair_scores(q, k):
    lane = lax.broadcasted_iota(jnp.int32, (1, PAIR), 1)
    scale = HD ** (-0.5)
    left = jnp.where(lane < HD, scale, 0.0).astype(BF16)
    right = jnp.where(lane < HD, 0.0, scale).astype(BF16)
    both = jnp.concatenate([q * left, q * right], axis=0)
    return lax.dot_general(both, k, (((1,), (1,)), ((), ())), preferred_element_type=F32)


def pair_expon(scores, bias):
    rows, keys = bias.shape
    scores = scores.reshape(2, rows, keys) + bias[None]
    highest = jnp.max(scores, axis=-1, keepdims=True)
    return jnp.exp(scores - highest).reshape(2 * rows, keys).astype(BF16)


def pair_mixed(expon, v):
    rows = expon.shape[0] // 2
    lane = lax.broadcasted_iota(jnp.int32, (1, PAIR), 1)
    mixed = jnp.dot(
        expon, jnp.concatenate([v, jnp.ones_like(v)], axis=1), preferred_element_type=F32
    )
    mixed = (mixed[:, :PAIR] * (1.0 / mixed[:, PAIR:])).reshape(2, rows, PAIR)
    return jnp.where(lane < HD, mixed[0], mixed[1]).astype(BF16)


def lanes_of(pair):
    return slice(pair * PAIR, (pair + 1) * PAIR)


def attention(query, key, value, store, bias_ref, scores_s, expon_s):
    for pair in range(H // 2):
        scores_s[pair] = pair_scores(query(lanes_of(pair)), key(lanes_of(pair)))
    for pair in range(H // 2):
        expon_s[pair] = pair_expon(scores_s[pair], bias_ref[...])
    for pair in range(H // 2):
        store(lanes_of(pair), pair_mixed(expon_s[pair], value(lanes_of(pair))))


def window_bias(start, reach_ref, count_ref, frame_len, total):
    row = lax.broadcasted_iota(jnp.int32, (BLK, WIN), 0)
    col = lax.broadcasted_iota(jnp.int32, (BLK, WIN), 1)
    distance = col - BLK - row
    reach = reach_ref[lax.div(jnp.clip(start, 0, total - 1), frame_len)]
    least = jnp.zeros((1, WIN), jnp.int32)
    place = lax.broadcasted_iota(jnp.int32, (1, WIN), 1)
    for j in range(3):
        at = start + (j - 1) * BLK
        inside = (at >= 0) & (at < total)
        frame = lax.div(jnp.clip(at, 0, total - 1), frame_len)
        first = (frame + 1) * frame_len - count_ref[frame] - at
        first = jnp.where(inside, first, WIN) + j * BLK
        least = jnp.where(place >= j * BLK, first, least)
    living = (col >= least) | (distance == 0)
    return jnp.where((jnp.abs(distance) <= reach) & living, 0.0, MASKED).astype(F32)


def space_attention(start, tables, q, k, v, mixed_s, bias_s, scores_s, expon_s):
    def load(what, length, i):
        ref, row, column = what
        rows = pl.ds(pl.multiple_of(row + i * BLK, BLK), length)
        return lambda lanes: ref[rows, column + lanes.start : column + lanes.stop]

    def one_block(i, carry):
        bias_s[...] = window_bias(start + i * BLK, *tables)
        rows = pl.ds(pl.multiple_of(i * BLK, BLK), BLK)

        def store(lanes, mixed):
            mixed_s[rows, lanes] = mixed

        attention(load(q, BLK, i), load(k, WIN, i), load(v, WIN, i), store, bias_s, scores_s, expon_s)
        return carry

    lax.fori_loop(0, 2, one_block, 0)


def times(x, weight):
    return jnp.dot(x, weight, preferred_element_type=F32)


def copies(sems, *pairs):
    made = [pltpu.make_async_copy(a, b, sems.at[i]) for i, (a, b) in enumerate(pairs)]
    for copy in made:
        copy.start()
    return made


QUERY, KEY, VALUE = slice(0, D), slice(D, 2 * D), slice(2 * D, 3 * D)


def middle_kernel(
    frame_len,
    total,
    reach_ref,
    count_ref,
    index_ref,
    gain_ref,
    x_hbm,
    project_hbm,
    output_hbm,
    first_hbm,
    state_hbm,
    second_hbm,
    x_s,
    project_s,
    output_s,
    first_s,
    state_s,
    second_s,
    mixed_s,
    bias_s,
    scores_s,
    expon_s,
    in_sems,
    out_sems,
):
    rows = x_s.shape[0]
    offset = index_ref[0] * rows
    gain = gain_ref[...]
    inner = slice(BLK, rows - BLK)
    x_in, query_in, key_in, value_in, output_in = copies(
        in_sems,
        (x_hbm, x_s),
        (project_hbm.at[:, QUERY], project_s.at[:, QUERY]),
        (project_hbm.at[:, KEY], project_s.at[:, KEY]),
        (project_hbm.at[:, VALUE], project_s.at[:, VALUE]),
        (output_hbm, output_s),
    )
    x_in.wait()
    hidden = norm_rows(x_s[...], gain)
    for copy, cols in ((query_in, QUERY), (key_in, KEY), (value_in, VALUE)):
        copy.wait()
        first_s[:, cols] = times(hidden, project_s[:, cols]).astype(BF16)
    first_out = pltpu.make_async_copy(first_s, first_hbm, out_sems.at[0])
    first_out.start()
    tables = (reach_ref, count_ref, frame_len, total)
    space_attention(
        offset + BLK,
        tables,
        (first_s, BLK, 0),
        (first_s, 0, D),
        (first_s, 0, 2 * D),
        mixed_s,
        bias_s,
        scores_s,
        expon_s,
    )
    output_in.wait()
    state_s[...] = (x_s[inner].astype(F32) + times(mixed_s[...], output_s[...])).astype(BF16)
    state_out = pltpu.make_async_copy(state_s, state_hbm, out_sems.at[1])
    state_out.start()
    hidden = norm_rows(state_s[...], gain)
    for cols in (QUERY, KEY, VALUE):
        second_s[:, cols] = times(hidden, project_s[:, cols]).astype(BF16)
    second_out = pltpu.make_async_copy(second_s, second_hbm, out_sems.at[2])
    second_out.start()
    first_out.wait()
    state_out.wait()
    second_out.wait()


def side_kernel(
    frame_len,
    total,
    after,
    reach_ref,
    count_ref,
    index_ref,
    gain_ref,
    time_gain_ref,
    halo_hbm,
    x_hbm,
    first_hbm,
    middle_hbm,
    second_hbm,
    project_hbm,
    output_hbm,
    state_ref,
    hidden_ref,
    halo_s,
    x_s,
    middle_s,
    project_s,
    output_s,
    q_s,
    k_s,
    v_s,
    q2_s,
    k2_s,
    v2_s,
    edge_s,
    mixed_s,
    bias_s,
    scores_s,
    expon_s,
    in_sems,
):
    local_rows = x_hbm.shape[0]
    offset = index_ref[0] * local_rows
    gain = gain_ref[...]
    half = 2 * BLK
    low, high = slice(0, BLK), slice(BLK, half)
    front, back = slice(0, half), slice(half, 2 * half)
    if after:
        begin = local_rows - half
        own_part, far_part = front, back
        mid_part, edge_part = front, back
        far_edge = low
        own_at, far_at = low, high
        mid_own, mid_at, edge_at = high, low, high
        start1, start2 = begin + BLK, begin
        own_rows = pl.ds(begin, half)
        edge_rows = pl.ds(local_rows - BLK, BLK)
    else:
        own_part, far_part = back, front
        mid_part, edge_part = back, front
        far_edge = high
        own_at, far_at = high, low
        mid_own, mid_at, edge_at = low, high, low
        start1, start2 = -BLK, 0
        own_rows = pl.ds(0, half)
        edge_rows = pl.ds(0, BLK)
    halo_in, key_in, value_in, query_in, k_in, v_in, q_in, output_in, x_in, k2_in, v2_in, q2_in, middle_in = copies(
        in_sems,
        (halo_hbm, halo_s),
        (project_hbm.at[:, KEY], project_s.at[:, KEY]),
        (project_hbm.at[:, VALUE], project_s.at[:, VALUE]),
        (project_hbm.at[:, QUERY], project_s.at[:, QUERY]),
        (first_hbm.at[own_rows, KEY], k_s.at[own_part]),
        (first_hbm.at[own_rows, VALUE], v_s.at[own_part]),
        (first_hbm.at[edge_rows, QUERY], q_s.at[own_at]),
        (output_hbm, output_s),
        (x_hbm.at[edge_rows], x_s),
        (second_hbm.at[:, KEY], k2_s.at[mid_part]),
        (second_hbm.at[:, VALUE], v2_s.at[mid_part]),
        (second_hbm.at[mid_own, QUERY], q2_s.at[mid_at]),
        (middle_hbm.at[mid_own], middle_s),
    )
    tables = (reach_ref, count_ref, frame_len, total)
    halo_in.wait()
    hidden = norm_rows(halo_s[...], gain)
    key_in.wait()
    k_s[far_part] = times(hidden, project_s[:, KEY]).astype(BF16)
    value_in.wait()
    v_s[far_part] = times(hidden, project_s[:, VALUE]).astype(BF16)
    query_in.wait()
    q_s[far_at] = times(hidden[far_edge], project_s[:, QUERY]).astype(BF16)
    k_in.wait()
    v_in.wait()
    q_in.wait()
    work = (mixed_s, bias_s, scores_s, expon_s)
    space_attention(offset + start1, tables, (q_s, 0, 0), (k_s, 0, 0), (v_s, 0, 0), *work)
    output_in.wait()
    x_in.wait()
    update = times(mixed_s[...], output_s[...])
    edge_s[own_at] = (x_s[...].astype(F32) + update[own_at]).astype(BF16)
    edge_s[far_at] = (halo_s[far_edge].astype(F32) + update[far_at]).astype(BF16)

    hidden = norm_rows(edge_s[...], gain)
    k2_s[edge_part] = times(hidden, project_s[:, KEY]).astype(BF16)
    v2_s[edge_part] = times(hidden, project_s[:, VALUE]).astype(BF16)
    q2_s[edge_at] = times(hidden[own_at], project_s[:, QUERY]).astype(BF16)
    k2_in.wait()
    v2_in.wait()
    q2_in.wait()
    space_attention(offset + start2, tables, (q2_s, 0, 0), (k2_s, 0, 0), (v2_s, 0, 0), *work)
    middle_in.wait()
    update = times(mixed_s[...], output_s[...])
    state_ref[edge_at] = (edge_s[own_at].astype(F32) + update[edge_at]).astype(BF16)
    state_ref[mid_at] = (middle_s[...].astype(F32) + update[mid_at]).astype(BF16)
    hidden_ref[...] = norm_rows(state_ref[...], time_gain_ref[...])


def time_kernel(
    frame_len,
    local_rows,
    devices,
    chunk,
    count_ref,
    index_ref,
    x_hbm,
    project_hbm,
    output_hbm,
    update_ref,
    x_s,
    project_s,
    output_s,
    qkv_s,
    mixed_s,
    bias_s,
    scores_s,
    expon_s,
    in_sems,
):
    rows = x_s.shape[0]
    slots = rows // F
    piece = rows // devices
    x_in, query_in, key_in, value_in, output_in = copies(
        in_sems,
        (x_hbm, x_s),
        (project_hbm.at[:, QUERY], project_s.at[:, QUERY]),
        (project_hbm.at[:, KEY], project_s.at[:, KEY]),
        (project_hbm.at[:, VALUE], project_s.at[:, VALUE]),
        (output_hbm, output_s),
    )
    row = lax.broadcasted_iota(jnp.int32, (rows, rows), 0)
    col = lax.broadcasted_iota(jnp.int32, (rows, rows), 1)
    key = lax.broadcasted_iota(jnp.int32, (1, rows), 1)
    key_frame = lax.div(key, slots)
    key_slot = lax.rem(key, slots)
    place = lax.div(key_slot, piece) * local_rows + lax.rem(key_slot, piece)
    place = place + chunk * rows + index_ref[0] * piece
    least = jnp.zeros((1, rows), jnp.int32)
    for g in range(F):
        least = jnp.where(key_frame == g, frame_len - count_ref[g], least)
    living = jnp.where(place >= least, 1, 0)
    same = lax.rem(row, slots) == lax.rem(col, slots)
    bias_s[...] = jnp.where(same & ((living == 1) | (row == col)), 0.0, MASKED).astype(F32)

    x_in.wait()
    for copy, cols in ((query_in, QUERY), (key_in, KEY), (value_in, VALUE)):
        copy.wait()
        qkv_s[:, cols] = times(x_s[...], project_s[:, cols]).astype(BF16)

    def columns(first):
        return lambda lanes: qkv_s[:, first + lanes.start : first + lanes.stop]

    def store(lanes, mixed):
        mixed_s[:, lanes] = mixed

    attention(columns(0), columns(D), columns(2 * D), store, bias_s, scores_s, expon_s)
    output_in.wait()
    update_ref[...] = times(mixed_s[...], output_s[...]).astype(BF16)


def smem():
    return pl.BlockSpec(memory_space=pltpu.SMEM)


def vmem():
    return pl.BlockSpec(memory_space=pltpu.VMEM)


def hbm():
    return pl.BlockSpec(memory_space=pl.ANY)


def rows16(rows, cols):
    return jax.ShapeDtypeStruct((rows, cols), BF16)


def scratch(rows, cols):
    return pltpu.VMEM((rows, cols), BF16)


def work(rows, keys):
    return [
        scratch(CHUNK, D),
        pltpu.VMEM((rows, keys), F32),
        pltpu.VMEM((H // 2, 2 * rows, keys), F32),
        pltpu.VMEM((H // 2, 2 * rows, keys), BF16),
    ]


def sems(count):
    return pltpu.SemaphoreType.DMA((count,))


def call(kernel, flops, exps, **rest):
    return pl.pallas_call(
        kernel,
        compiler_params=pltpu.CompilerParams(vmem_limit_bytes=VMEM_LIMIT),
        cost_estimate=pl.CostEstimate(
            flops=flops, bytes_accessed=16 * D * D, transcendentals=exps
        ),
        **rest,
    )


def on_device(
    frame_tokens,
    window_reach,
    valid_count,
    space_gain,
    space_project,
    space_output,
    time_gain,
    time_project,
    time_output,
):
    devices = lax.axis_size("strip")
    local_rows = frame_tokens.shape[0]
    total = local_rows * devices
    frame_len = total // F
    if local_rows != 2 * CHUNK or frame_len % local_rows or CHUNK % devices:
        raise ValueError("unsupported sizes")
    index = lax.axis_index("strip").reshape(1)
    gain = space_gain.reshape(1, D)
    gain_t = time_gain.reshape(1, D)

    up = [(i, i + 1) for i in range(devices - 1)]
    down = [(i + 1, i) for i in range(devices - 1)]
    before = lax.ppermute(frame_tokens[local_rows - CHUNK :], "strip", up)
    after = lax.ppermute(frame_tokens[:CHUNK], "strip", down)

    first, middle, second = call(
        functools.partial(middle_kernel, frame_len, total),
        2 * D * D * 10 * CHUNK,
        H * CHUNK * WIN,
        out_shape=(rows16(local_rows, 3 * D), rows16(CHUNK, D), rows16(CHUNK, 3 * D)),
        in_specs=[smem()] * 3 + [vmem()] + [hbm()] * 3,
        out_specs=(hbm(),) * 3,
        scratch_shapes=[
            scratch(local_rows, D),
            scratch(D, 3 * D),
            scratch(D, D),
            scratch(local_rows, 3 * D),
            scratch(CHUNK, D),
            scratch(CHUNK, 3 * D),
            *work(BLK, WIN),
            sems(5),
            sems(3),
        ],
    )(window_reach, valid_count, index, gain, frame_tokens, space_project, space_output)

    def side(halo, is_after):
        return call(
            functools.partial(side_kernel, frame_len, total, is_after),
            2 * D * D * 10 * CHUNK,
            2 * H * CHUNK * WIN,
            out_shape=(rows16(CHUNK, D),) * 2,
            in_specs=[smem()] * 3 + [vmem()] * 2 + [hbm()] * 7,
            out_specs=(vmem(),) * 2,
            scratch_shapes=[
                scratch(CHUNK, D),
                scratch(BLK, D),
                scratch(BLK, D),
                scratch(D, 3 * D),
                scratch(D, D),
                scratch(CHUNK, D),
                scratch(2 * CHUNK, D),
                scratch(2 * CHUNK, D),
                scratch(CHUNK, D),
                scratch(2 * CHUNK, D),
                scratch(2 * CHUNK, D),
                scratch(CHUNK, D),
                *work(BLK, WIN),
                sems(13),
            ],
        )(
            window_reach,
            valid_count,
            index,
            gain,
            gain_t,
            halo,
            frame_tokens,
            first,
            middle,
            second,
            space_project,
            space_output,
        )

    def exchange(x):
        return lax.all_to_all(x, "strip", split_axis=0, concat_axis=0, tiled=True)

    def temporal(x, chunk):
        return call(
            functools.partial(time_kernel, frame_len, local_rows, devices, chunk),
            2 * D * D * 5 * CHUNK,
            H * CHUNK * CHUNK,
            out_shape=rows16(CHUNK, D),
            in_specs=[smem()] * 2 + [hbm()] * 3,
            out_specs=vmem(),
            scratch_shapes=[
                scratch(CHUNK, D),
                scratch(D, 3 * D),
                scratch(D, D),
                scratch(CHUNK, 3 * D),
                *work(CHUNK, CHUNK),
                sems(5),
            ],
        )(valid_count, index, x, time_project, time_output)

    state0, hidden0 = side(before, False)
    sent0 = exchange(hidden0)
    state1, hidden1 = side(after, True)
    sent1 = exchange(hidden1)
    back0 = exchange(temporal(sent0, 0))
    back1 = exchange(temporal(sent1, 1))
    wide = [
        (s.astype(F32) + b.astype(F32)).astype(BF16) for s, b in ((state0, back0), (state1, back1))
    ]
    return jnp.concatenate(wide, axis=0)


def solution(mesh):
    return jax.shard_map(
        on_device,
        mesh=mesh,
        in_specs=(
            P(("group", "strip"), None),
            P("group"),
            P("group"),
            P(),
            P(),
            P(),
            P(),
            P(),
            P(),
        ),
        out_specs=P(("group", "strip"), None),
        check_vma=False,
    )
```

```python
import functools

import jax
import jax.numpy as jnp
from jax import lax
from jax.experimental import pallas as pl
from jax.experimental.pallas import tpu as pltpu
from jax.sharding import PartitionSpec as P


F = 16
HALO = 128
H = 12
HD = 64
D = 768
BLK = HALO
WIN = 3 * BLK
PAIR = 2 * HD
CHUNK = 2 * BLK
VMEM_LIMIT = 60 * 1024 * 1024
ROOMY = 56 << 20
EPS = 1e-06
MASKED = -1e30

BF16 = jnp.bfloat16
F32 = jnp.float32


def norm_rows(values, gain):
    wide = values.astype(F32)
    meansq = jnp.mean(wide * wide, axis=-1, keepdims=True)
    return (wide * lax.rsqrt(meansq + EPS) * gain.reshape(1, D)).astype(BF16)


def pair_scores(q, k):
    lane = lax.broadcasted_iota(jnp.int32, (1, PAIR), 1)
    scale = HD ** (-0.5)
    left = jnp.where(lane < HD, scale, 0.0).astype(BF16)
    right = jnp.where(lane < HD, 0.0, scale).astype(BF16)
    both = jnp.concatenate([q * left, q * right], axis=0)
    return lax.dot_general(both, k, (((1,), (1,)), ((), ())), preferred_element_type=F32)


def pair_expon(scores, bias):
    rows, keys = bias.shape
    scores = scores.reshape(2, rows, keys) + bias[None]
    highest = jnp.max(scores, axis=-1, keepdims=True)
    return jnp.exp(scores - highest).reshape(2 * rows, keys).astype(BF16)


def pair_mixed(expon, v):
    rows = expon.shape[0] // 2
    lane = lax.broadcasted_iota(jnp.int32, (1, PAIR), 1)
    mixed = jnp.dot(
        expon, jnp.concatenate([v, jnp.ones_like(v)], axis=1), preferred_element_type=F32
    )
    mixed = (mixed[:, :PAIR] * (1.0 / mixed[:, PAIR:])).reshape(2, rows, PAIR)
    return jnp.where(lane < HD, mixed[0], mixed[1]).astype(BF16)


def lanes_of(pair):
    return slice(pair * PAIR, (pair + 1) * PAIR)


def attention(query, key, value, store, bias_ref, scores_s, expon_s):
    for pair in range(H // 2):
        scores_s[pair] = pair_scores(query(lanes_of(pair)), key(lanes_of(pair)))
    for pair in range(H // 2):
        expon_s[pair] = pair_expon(scores_s[pair], bias_ref[...])
    for pair in range(H // 2):
        store(lanes_of(pair), pair_mixed(expon_s[pair], value(lanes_of(pair))))


def window_bias(start, reach_ref, count_ref, frame_len, total):
    row = lax.broadcasted_iota(jnp.int32, (BLK, WIN), 0)
    col = lax.broadcasted_iota(jnp.int32, (BLK, WIN), 1)
    distance = col - BLK - row
    reach = reach_ref[lax.div(jnp.clip(start, 0, total - 1), frame_len)]
    least = jnp.zeros((1, WIN), jnp.int32)
    place = lax.broadcasted_iota(jnp.int32, (1, WIN), 1)
    for j in range(3):
        at = start + (j - 1) * BLK
        inside = (at >= 0) & (at < total)
        frame = lax.div(jnp.clip(at, 0, total - 1), frame_len)
        first = (frame + 1) * frame_len - count_ref[frame] - at
        first = jnp.where(inside, first, WIN) + j * BLK
        least = jnp.where(place >= j * BLK, first, least)
    living = (col >= least) | (distance == 0)
    return jnp.where((jnp.abs(distance) <= reach) & living, 0.0, MASKED).astype(F32)


def space_attention(start, tables, q, k, v, mixed_s, bias_s, scores_s, expon_s):
    def load(what, length, i):
        ref, row, column = what
        rows = pl.ds(pl.multiple_of(row + i * BLK, BLK), length)
        return lambda lanes: ref[rows, column + lanes.start : column + lanes.stop]

    def one_block(i, carry):
        bias_s[...] = window_bias(start + i * BLK, *tables)
        rows = pl.ds(pl.multiple_of(i * BLK, BLK), BLK)

        def store(lanes, mixed):
            mixed_s[rows, lanes] = mixed

        attention(load(q, BLK, i), load(k, WIN, i), load(v, WIN, i), store, bias_s, scores_s, expon_s)
        return carry

    lax.fori_loop(0, 2, one_block, 0)


def times(x, weight):
    return jnp.dot(x, weight, preferred_element_type=F32)


def copies(sems, *pairs):
    made = [pltpu.make_async_copy(a, b, sems.at[i]) for i, (a, b) in enumerate(pairs)]
    for copy in made:
        copy.start()
    return made


QUERY, KEY, VALUE = slice(0, D), slice(D, 2 * D), slice(2 * D, 3 * D)


def middle_kernel(
    frame_len,
    total,
    reach_ref,
    count_ref,
    index_ref,
    gain_ref,
    x_hbm,
    project_hbm,
    output_hbm,
    first0_hbm,
    state0_hbm,
    second0_hbm,
    query0_hbm,
    first1_hbm,
    state1_hbm,
    second1_hbm,
    query1_hbm,
    x_s,
    project_s,
    output_s,
    first_s,
    state_s,
    second_s,
    mixed_s,
    bias_s,
    scores_s,
    expon_s,
    in_sems,
    out_sems,
):
    rows = x_s.shape[0]
    offset = index_ref[0] * rows
    gain = gain_ref[...]
    inner = slice(BLK, rows - BLK)
    x_in, query_in, key_in, value_in, output_in = copies(
        in_sems,
        (x_hbm, x_s),
        (project_hbm.at[:, QUERY], project_s.at[:, QUERY]),
        (project_hbm.at[:, KEY], project_s.at[:, KEY]),
        (project_hbm.at[:, VALUE], project_s.at[:, VALUE]),
        (output_hbm, output_s),
    )
    x_in.wait()
    hidden = norm_rows(x_s[...], gain)
    for copy, cols in ((query_in, QUERY), (key_in, KEY), (value_in, VALUE)):
        copy.wait()
        first_s[:, cols] = times(hidden, project_s[:, cols]).astype(BF16)
    half = 2 * BLK
    out = copies(out_sems.at[0:2], (first_s.at[:half], first0_hbm), (first_s.at[half:], first1_hbm))
    tables = (reach_ref, count_ref, frame_len, total)
    space_attention(
        offset + BLK,
        tables,
        (first_s, BLK, 0),
        (first_s, 0, D),
        (first_s, 0, 2 * D),
        mixed_s,
        bias_s,
        scores_s,
        expon_s,
    )
    output_in.wait()
    state_s[...] = (x_s[inner].astype(F32) + times(mixed_s[...], output_s[...])).astype(BF16)
    out += copies(out_sems.at[2:4], (state_s.at[:BLK], state0_hbm), (state_s.at[BLK:], state1_hbm))
    hidden = norm_rows(state_s[...], gain)
    for cols in (QUERY, KEY, VALUE):
        second_s[:, cols] = times(hidden, project_s[:, cols]).astype(BF16)
    out += copies(
        out_sems.at[4:8],
        (second_s.at[:, D:], second0_hbm),
        (second_s.at[:, D:], second1_hbm),
        (second_s.at[:BLK, QUERY], query0_hbm),
        (second_s.at[BLK:, QUERY], query1_hbm),
    )
    for copy in out:
        copy.wait()


def side_kernel(
    frame_len,
    total,
    after,
    reach_ref,
    count_ref,
    index_ref,
    gain_ref,
    time_gain_ref,
    halo_hbm,
    x_hbm,
    first_hbm,
    middle_hbm,
    second_hbm,
    query2_hbm,
    project_hbm,
    output_hbm,
    state_ref,
    hidden_ref,
    halo_s,
    x_s,
    middle_s,
    project_s,
    output_s,
    q_s,
    k_s,
    v_s,
    q2_s,
    k2_s,
    v2_s,
    edge_s,
    mixed_s,
    bias_s,
    scores_s,
    expon_s,
    in_sems,
):
    local_rows = x_hbm.shape[0]
    offset = index_ref[0] * local_rows
    gain = gain_ref[...]
    half = 2 * BLK
    low, high = slice(0, BLK), slice(BLK, half)
    front, back = slice(0, half), slice(half, 2 * half)
    if after:
        begin = local_rows - half
        own_part, far_part = front, back
        mid_part, edge_part = front, back
        own_edge, far_edge = high, low
        own_at, far_at = low, high
        mid_at, edge_at = low, high
        start1, start2 = begin + BLK, begin
        edge_rows = pl.ds(local_rows - BLK, BLK)
    else:
        own_part, far_part = back, front
        mid_part, edge_part = back, front
        own_edge, far_edge = low, high
        own_at, far_at = high, low
        mid_at, edge_at = high, low
        start1, start2 = -BLK, 0
        edge_rows = pl.ds(0, BLK)
    halo_in, key_in, value_in, query_in, k_in, v_in, q_in, output_in, x_in, k2_in, v2_in, q2_in, middle_in = copies(
        in_sems,
        (halo_hbm, halo_s),
        (project_hbm.at[:, KEY], project_s.at[:, KEY]),
        (project_hbm.at[:, VALUE], project_s.at[:, VALUE]),
        (project_hbm.at[:, QUERY], project_s.at[:, QUERY]),
        (first_hbm.at[:, KEY], k_s.at[own_part]),
        (first_hbm.at[:, VALUE], v_s.at[own_part]),
        (first_hbm.at[own_edge, QUERY], q_s.at[own_at]),
        (output_hbm, output_s),
        (x_hbm.at[edge_rows], x_s),
        (second_hbm.at[:, :D], k2_s.at[mid_part]),
        (second_hbm.at[:, D:], v2_s.at[mid_part]),
        (query2_hbm, q2_s.at[mid_at]),
        (middle_hbm, middle_s),
    )
    tables = (reach_ref, count_ref, frame_len, total)
    halo_in.wait()
    hidden = norm_rows(halo_s[...], gain)
    key_in.wait()
    k_s[far_part] = times(hidden, project_s[:, KEY]).astype(BF16)
    value_in.wait()
    v_s[far_part] = times(hidden, project_s[:, VALUE]).astype(BF16)
    query_in.wait()
    q_s[far_at] = times(hidden[far_edge], project_s[:, QUERY]).astype(BF16)
    k_in.wait()
    v_in.wait()
    q_in.wait()
    work = (mixed_s, bias_s, scores_s, expon_s)
    space_attention(offset + start1, tables, (q_s, 0, 0), (k_s, 0, 0), (v_s, 0, 0), *work)
    output_in.wait()
    x_in.wait()
    update = times(mixed_s[...], output_s[...])
    edge_s[own_at] = (x_s[...].astype(F32) + update[own_at]).astype(BF16)
    edge_s[far_at] = (halo_s[far_edge].astype(F32) + update[far_at]).astype(BF16)

    hidden = norm_rows(edge_s[...], gain)
    k2_s[edge_part] = times(hidden, project_s[:, KEY]).astype(BF16)
    v2_s[edge_part] = times(hidden, project_s[:, VALUE]).astype(BF16)
    q2_s[edge_at] = times(hidden[own_at], project_s[:, QUERY]).astype(BF16)
    k2_in.wait()
    v2_in.wait()
    q2_in.wait()
    space_attention(offset + start2, tables, (q2_s, 0, 0), (k2_s, 0, 0), (v2_s, 0, 0), *work)
    middle_in.wait()
    update = times(mixed_s[...], output_s[...])
    state_ref[edge_at] = (edge_s[own_at].astype(F32) + update[edge_at]).astype(BF16)
    state_ref[mid_at] = (middle_s[...].astype(F32) + update[mid_at]).astype(BF16)
    hidden_ref[...] = norm_rows(state_ref[...], time_gain_ref[...])


def time_kernel(
    frame_len,
    local_rows,
    devices,
    chunk,
    merged,
    count_ref,
    index_ref,
    x_hbm,
    project_hbm,
    output_hbm,
    *rest,
):
    other_hbm = rest[0] if merged else None
    (
        update_ref,
        x_s,
        project_s,
        output_s,
        qkv_s,
        mixed_s,
        bias_s,
        scores_s,
        expon_s,
        in_sems,
    ) = rest[1 if merged else 0 :][:10]
    other_s = rest[-1]
    rows = x_s.shape[0]
    slots = rows // F
    piece = rows // devices
    others = [(other_hbm, other_s)] if merged else []
    x_in, query_in, key_in, value_in, output_in, *other_in = copies(
        in_sems,
        (x_hbm, x_s),
        (project_hbm.at[:, QUERY], project_s.at[:, QUERY]),
        (project_hbm.at[:, KEY], project_s.at[:, KEY]),
        (project_hbm.at[:, VALUE], project_s.at[:, VALUE]),
        (output_hbm, output_s),
        *others,
    )
    row = lax.broadcasted_iota(jnp.int32, (rows, rows), 0)
    col = lax.broadcasted_iota(jnp.int32, (rows, rows), 1)
    key = lax.broadcasted_iota(jnp.int32, (1, rows), 1)
    key_frame = lax.div(key, slots)
    key_slot = lax.rem(key, slots)
    place = lax.div(key_slot, piece) * local_rows + lax.rem(key_slot, piece)
    place = place + chunk * rows + index_ref[0] * piece
    least = jnp.zeros((1, rows), jnp.int32)
    for g in range(F):
        least = jnp.where(key_frame == g, frame_len - count_ref[g], least)
    living = jnp.where(place >= least, 1, 0)
    same = lax.rem(row, slots) == lax.rem(col, slots)
    bias_s[...] = jnp.where(same & ((living == 1) | (row == col)), 0.0, MASKED).astype(F32)

    x_in.wait()
    for copy, cols in ((query_in, QUERY), (key_in, KEY), (value_in, VALUE)):
        copy.wait()
        qkv_s[:, cols] = times(x_s[...], project_s[:, cols]).astype(BF16)

    def columns(first):
        return lambda lanes: qkv_s[:, first + lanes.start : first + lanes.stop]

    def store(lanes, mixed):
        mixed_s[:, lanes] = mixed

    attention(columns(0), columns(D), columns(2 * D), store, bias_s, scores_s, expon_s)
    output_in.wait()
    update = times(mixed_s[...], output_s[...]).astype(BF16)
    if not merged:
        update_ref[...] = update
        return
    other_in[0].wait()
    for device in range(devices):
        part = slice(device * piece, (device + 1) * piece)
        place = 2 * device * piece
        update_ref[place : place + piece] = other_s[part]
        update_ref[place + piece : place + 2 * piece] = update[part]


def smem():
    return pl.BlockSpec(memory_space=pltpu.SMEM)


def vmem():
    return pl.BlockSpec(memory_space=pltpu.VMEM)


def hbm():
    return pl.BlockSpec(memory_space=pl.ANY)


def rows16(rows, cols):
    return jax.ShapeDtypeStruct((rows, cols), BF16)


def scratch(rows, cols):
    return pltpu.VMEM((rows, cols), BF16)


def work(rows, keys):
    return [
        scratch(CHUNK, D),
        pltpu.VMEM((rows, keys), F32),
        pltpu.VMEM((H // 2, 2 * rows, keys), F32),
        pltpu.VMEM((H // 2, 2 * rows, keys), BF16),
    ]


def sems(count):
    return pltpu.SemaphoreType.DMA((count,))


def call(kernel, flops, exps, limit=VMEM_LIMIT, **rest):
    return pl.pallas_call(
        kernel,
        compiler_params=pltpu.CompilerParams(vmem_limit_bytes=limit),
        cost_estimate=pl.CostEstimate(
            flops=flops, bytes_accessed=16 * D * D, transcendentals=exps
        ),
        **rest,
    )


def on_device(
    frame_tokens,
    window_reach,
    valid_count,
    space_gain,
    space_project,
    space_output,
    time_gain,
    time_project,
    time_output,
):
    devices = lax.axis_size("strip")
    local_rows = frame_tokens.shape[0]
    total = local_rows * devices
    frame_len = total // F
    if local_rows != 2 * CHUNK or frame_len % local_rows or CHUNK % devices:
        raise ValueError("unsupported sizes")
    index = lax.axis_index("strip").reshape(1)
    piece = CHUNK // devices

    up = [(i, i + 1) for i in range(devices - 1)]
    down = [(i + 1, i) for i in range(devices - 1)]
    before = lax.ppermute(frame_tokens[local_rows - CHUNK :], "strip", up)
    after = lax.ppermute(frame_tokens[:CHUNK], "strip", down)

    sides = call(
        functools.partial(middle_kernel, frame_len, total),
        2 * D * D * 10 * CHUNK,
        H * CHUNK * WIN,
        limit=ROOMY,
        out_shape=(
            rows16(CHUNK, 3 * D),
            rows16(BLK, D),
            rows16(CHUNK, 2 * D),
            rows16(BLK, D),
        )
        * 2,
        in_specs=[smem()] * 3 + [vmem()] + [hbm()] * 3,
        out_specs=(hbm(),) * 8,
        scratch_shapes=[
            scratch(local_rows, D),
            scratch(D, 3 * D),
            scratch(D, D),
            scratch(local_rows, 3 * D),
            scratch(CHUNK, D),
            scratch(CHUNK, 3 * D),
            *work(BLK, WIN),
            sems(5),
            sems(8),
        ],
    )(window_reach, valid_count, index, space_gain, frame_tokens, space_project, space_output)

    def side(halo, is_after):
        return call(
            functools.partial(side_kernel, frame_len, total, is_after),
            2 * D * D * 10 * CHUNK,
            2 * H * CHUNK * WIN,
            out_shape=(rows16(CHUNK, D),) * 2,
            limit=VMEM_LIMIT if is_after else ROOMY,
            in_specs=[smem()] * 3 + [vmem()] * 2 + [hbm()] * 8,
            out_specs=(vmem(),) * 2,
            scratch_shapes=[
                scratch(CHUNK, D),
                scratch(BLK, D),
                scratch(BLK, D),
                scratch(D, 3 * D),
                scratch(D, D),
                scratch(CHUNK, D),
                scratch(2 * CHUNK, D),
                scratch(2 * CHUNK, D),
                scratch(CHUNK, D),
                scratch(2 * CHUNK, D),
                scratch(2 * CHUNK, D),
                scratch(CHUNK, D),
                *work(BLK, WIN),
                sems(13),
            ],
        )(
            window_reach,
            valid_count,
            index,
            space_gain,
            time_gain,
            halo,
            frame_tokens,
            *(sides[4:] if is_after else sides[:4]),
            space_project,
            space_output,
        )

    def exchange(x):
        return lax.all_to_all(x, "strip", split_axis=0, concat_axis=0, tiled=True)

    def temporal(x, chunk, *other):
        merged = len(other) > 0
        return call(
            functools.partial(time_kernel, frame_len, local_rows, devices, chunk, merged),
            2 * D * D * 5 * CHUNK,
            H * CHUNK * CHUNK,
            out_shape=rows16(2 * CHUNK if merged else CHUNK, D),
            in_specs=[smem()] * 2 + [hbm()] * (3 + len(other)),
            out_specs=vmem(),
            scratch_shapes=[
                scratch(CHUNK, D),
                scratch(D, 3 * D),
                scratch(D, D),
                scratch(CHUNK, 3 * D),
                *work(CHUNK, CHUNK),
                sems(5 + len(other)),
                *[scratch(CHUNK, D)] * len(other),
            ],
        )(valid_count, index, x, time_project, time_output, *other)

    state0, hidden0 = side(before, False)
    sent0 = exchange(hidden0)
    state1, hidden1 = side(after, True)
    sent1 = exchange(hidden1)
    update0 = temporal(sent0, 0)
    if piece % 8:
        back0 = exchange(update0)
        back1 = exchange(temporal(sent1, 1))
    else:
        back = exchange(temporal(sent1, 1, update0)).reshape(devices, 2, piece, D)
        back0, back1 = back[:, 0].reshape(CHUNK, D), back[:, 1].reshape(CHUNK, D)
    wide = [
        (s.astype(F32) + b.astype(F32)).astype(BF16) for s, b in ((state0, back0), (state1, back1))
    ]
    return jnp.concatenate(wide, axis=0)


def solution(mesh):
    return jax.shard_map(
        on_device,
        mesh=mesh,
        in_specs=(
            P(("group", "strip"), None),
            P("group"),
            P("group"),
            P(),
            P(),
            P(),
            P(),
            P(),
            P(),
        ),
        out_specs=P(("group", "strip"), None),
        check_vma=False,
    )
```

```python
import functools

import jax
import jax.numpy as jnp
from jax import lax
from jax.experimental import pallas as pl
from jax.experimental.pallas import tpu as pltpu
from jax.sharding import PartitionSpec as P


F = 16
HALO = 128
H = 12
HD = 64
D = 768
BLK = HALO
WIN = 3 * BLK
PAIR = 2 * HD
CHUNK = 2 * BLK
VMEM_LIMIT = 60 * 1024 * 1024
EPS = 1e-06
MASKED = -1e30

BF16 = jnp.bfloat16
F32 = jnp.float32


def norm_rows(values, gain):
    wide = values.astype(F32)
    meansq = jnp.mean(wide * wide, axis=-1, keepdims=True)
    return (wide * lax.rsqrt(meansq + EPS) * gain.reshape(1, D)).astype(BF16)


def pair_scores(q, k):
    lane = lax.broadcasted_iota(jnp.int32, (1, PAIR), 1)
    scale = HD ** (-0.5)
    left = jnp.where(lane < HD, scale, 0.0).astype(BF16)
    right = jnp.where(lane < HD, 0.0, scale).astype(BF16)
    both = jnp.concatenate([q * left, q * right], axis=0)
    return lax.dot_general(both, k, (((1,), (1,)), ((), ())), preferred_element_type=F32)


def pair_expon(scores, bias):
    rows, keys = bias.shape
    scores = scores.reshape(2, rows, keys) + bias[None]
    highest = jnp.max(scores, axis=-1, keepdims=True)
    return jnp.exp(scores - highest).reshape(2 * rows, keys).astype(BF16)


def pair_mixed(expon, v):
    rows = expon.shape[0] // 2
    lane = lax.broadcasted_iota(jnp.int32, (1, PAIR), 1)
    mixed = jnp.dot(
        expon, jnp.concatenate([v, jnp.ones_like(v)], axis=1), preferred_element_type=F32
    )
    mixed = (mixed[:, :PAIR] * (1.0 / mixed[:, PAIR:])).reshape(2, rows, PAIR)
    return jnp.where(lane < HD, mixed[0], mixed[1]).astype(BF16)


def lanes_of(pair):
    return slice(pair * PAIR, (pair + 1) * PAIR)


def attention(query, key, value, store, bias_ref, scores_s, expon_s):
    for pair in range(H // 2):
        scores_s[pair] = pair_scores(query(lanes_of(pair)), key(lanes_of(pair)))
    for pair in range(H // 2):
        expon_s[pair] = pair_expon(scores_s[pair], bias_ref[...])
    for pair in range(H // 2):
        store(lanes_of(pair), pair_mixed(expon_s[pair], value(lanes_of(pair))))


def window_bias(start, reach_ref, count_ref, frame_len, total):
    row = lax.broadcasted_iota(jnp.int32, (BLK, WIN), 0)
    col = lax.broadcasted_iota(jnp.int32, (BLK, WIN), 1)
    distance = col - BLK - row
    reach = reach_ref[lax.div(jnp.clip(start, 0, total - 1), frame_len)]
    least = jnp.zeros((1, WIN), jnp.int32)
    place = lax.broadcasted_iota(jnp.int32, (1, WIN), 1)
    for j in range(3):
        at = start + (j - 1) * BLK
        inside = (at >= 0) & (at < total)
        frame = lax.div(jnp.clip(at, 0, total - 1), frame_len)
        first = (frame + 1) * frame_len - count_ref[frame] - at
        first = jnp.where(inside, first, WIN) + j * BLK
        least = jnp.where(place >= j * BLK, first, least)
    living = (col >= least) | (distance == 0)
    return jnp.where((jnp.abs(distance) <= reach) & living, 0.0, MASKED).astype(F32)


def space_attention(blocks, start_of, window_of, tables, q, k, v, mixed_s, bias_s, scores_s, expon_s):
    def load(what, at, length):
        ref, row, column = what
        rows = pl.ds(pl.multiple_of(row + at, BLK), length)
        return lambda lanes: ref[rows, column + lanes.start : column + lanes.stop]

    def one_block(i, carry):
        bias_s[...] = window_bias(start_of(i), *tables)
        rows = pl.ds(pl.multiple_of(i * BLK, BLK), BLK)

        def store(lanes, mixed):
            mixed_s[rows, lanes] = mixed

        attention(
            load(q, i * BLK, BLK),
            load(k, window_of(i), WIN),
            load(v, window_of(i), WIN),
            store,
            bias_s,
            scores_s,
            expon_s,
        )
        return carry

    lax.fori_loop(0, blocks, one_block, 0)


def times(x, weight):
    return jnp.dot(x, weight, preferred_element_type=F32)


def copies(sems, *pairs):
    made = [pltpu.make_async_copy(a, b, sems.at[i]) for i, (a, b) in enumerate(pairs)]
    for copy in made:
        copy.start()
    return made


QUERY, KEY, VALUE = slice(0, D), slice(D, 2 * D), slice(2 * D, 3 * D)


def middle_kernel(
    frame_len,
    total,
    reach_ref,
    count_ref,
    index_ref,
    gain_ref,
    x_hbm,
    project_hbm,
    output_hbm,
    first_hbm,
    state_hbm,
    second_hbm,
    x_s,
    project_s,
    output_s,
    first_s,
    state_s,
    second_s,
    mixed_s,
    bias_s,
    scores_s,
    expon_s,
    in_sems,
    out_sems,
):
    rows = x_s.shape[0]
    offset = index_ref[0] * rows
    gain = gain_ref[...]
    inner = slice(BLK, rows - BLK)
    x_in, query_in, key_in, value_in, output_in = copies(
        in_sems,
        (x_hbm, x_s),
        (project_hbm.at[:, QUERY], project_s.at[:, QUERY]),
        (project_hbm.at[:, KEY], project_s.at[:, KEY]),
        (project_hbm.at[:, VALUE], project_s.at[:, VALUE]),
        (output_hbm, output_s),
    )
    x_in.wait()
    hidden = norm_rows(x_s[...], gain)
    for copy, cols in ((query_in, QUERY), (key_in, KEY), (value_in, VALUE)):
        copy.wait()
        first_s[:, cols] = times(hidden, project_s[:, cols]).astype(BF16)
    first_out = pltpu.make_async_copy(first_s, first_hbm, out_sems.at[0])
    first_out.start()
    tables = (reach_ref, count_ref, frame_len, total)
    space_attention(
        2,
        lambda i: offset + (i + 1) * BLK,
        lambda i: i * BLK,
        tables,
        (first_s, BLK, 0),
        (first_s, 0, D),
        (first_s, 0, 2 * D),
        mixed_s,
        bias_s,
        scores_s,
        expon_s,
    )
    output_in.wait()
    state_s[...] = (x_s[inner].astype(F32) + times(mixed_s[...], output_s[...])).astype(BF16)
    state_out = pltpu.make_async_copy(state_s, state_hbm, out_sems.at[1])
    state_out.start()
    hidden = norm_rows(state_s[...], gain)
    for cols in (QUERY, KEY, VALUE):
        second_s[:, cols] = times(hidden, project_s[:, cols]).astype(BF16)
    second_out = pltpu.make_async_copy(second_s, second_hbm, out_sems.at[2])
    second_out.start()
    first_out.wait()
    state_out.wait()
    second_out.wait()


def sides_kernel(
    frame_len,
    total,
    reach_ref,
    count_ref,
    index_ref,
    gain_ref,
    time_gain_ref,
    before_hbm,
    after_hbm,
    x_hbm,
    first_hbm,
    middle_hbm,
    second_hbm,
    project_hbm,
    output_hbm,
    state_ref,
    hidden_ref,
    halo_s,
    edge_s,
    middle_s,
    project_s,
    output_s,
    q_s,
    k_s,
    v_s,
    q2_s,
    k2_s,
    v2_s,
    mixed_s,
    bias_s,
    scores_s,
    expon_s,
    in_sems,
):
    rows = x_hbm.shape[0]
    offset = index_ref[0] * rows
    gain = gain_ref[...]
    half = 2 * BLK

    def block(first, last=None):
        return slice(first * BLK, (first + 1 if last is None else last) * BLK)

    (
        before_in,
        after_in,
        key_in,
        value_in,
        query_in,
        k_in,
        v_in,
        q_low_in,
        q_high_in,
        output_in,
        x_low_in,
        x_high_in,
        k2_in,
        v2_in,
        q2_in,
        middle_in,
    ) = copies(
        in_sems,
        (before_hbm, halo_s.at[block(0, 2)]),
        (after_hbm, halo_s.at[block(2, 4)]),
        (project_hbm.at[:, KEY], project_s.at[:, KEY]),
        (project_hbm.at[:, VALUE], project_s.at[:, VALUE]),
        (project_hbm.at[:, QUERY], project_s.at[:, QUERY]),
        (first_hbm.at[:, KEY], k_s.at[block(2, 6)]),
        (first_hbm.at[:, VALUE], v_s.at[block(2, 6)]),
        (first_hbm.at[block(0), QUERY], q_s.at[block(1)]),
        (first_hbm.at[block(3), QUERY], q_s.at[block(2)]),
        (output_hbm, output_s),
        (x_hbm.at[block(0)], edge_s.at[block(1)]),
        (x_hbm.at[block(3)], edge_s.at[block(2)]),
        (second_hbm.at[:, KEY], k2_s.at[block(2, 4)]),
        (second_hbm.at[:, VALUE], v2_s.at[block(2, 4)]),
        (second_hbm.at[:, QUERY], q2_s.at[block(1, 3)]),
        (middle_hbm, middle_s),
    )
    tables = (reach_ref, count_ref, frame_len, total)
    work = (mixed_s, bias_s, scores_s, expon_s)
    before_in.wait()
    after_in.wait()
    hidden = norm_rows(halo_s[...], gain)
    for copy, cols, ref in ((key_in, KEY, k_s), (value_in, VALUE, v_s)):
        copy.wait()
        made = times(hidden, project_s[:, cols]).astype(BF16)
        ref[block(0, 2)] = made[:half]
        ref[block(6, 8)] = made[half:]
    query_in.wait()
    made = times(hidden[block(1, 3)], project_s[:, QUERY]).astype(BF16)
    q_s[block(0)] = made[:BLK]
    q_s[block(3)] = made[BLK:]
    for copy in (k_in, v_in, q_low_in, q_high_in):
        copy.wait()

    def skip(i):
        return jnp.where(i >= 2, half, 0)

    space_attention(
        4,
        lambda i: offset + (i - 1) * BLK + skip(i),
        lambda i: i * BLK + skip(i),
        tables,
        (q_s, 0, 0),
        (k_s, 0, 0),
        (v_s, 0, 0),
        *work,
    )
    output_in.wait()
    x_low_in.wait()
    x_high_in.wait()
    update = times(mixed_s[...], output_s[...])
    edge_s[block(0)] = (halo_s[block(1)].astype(F32) + update[block(0)]).astype(BF16)
    edge_s[block(1, 3)] = (edge_s[block(1, 3)].astype(F32) + update[block(1, 3)]).astype(BF16)
    edge_s[block(3)] = (halo_s[block(2)].astype(F32) + update[block(3)]).astype(BF16)

    hidden = norm_rows(edge_s[...], gain)
    for cols, ref in ((KEY, k2_s), (VALUE, v2_s)):
        made = times(hidden, project_s[:, cols]).astype(BF16)
        ref[block(0, 2)] = made[:half]
        ref[block(4, 6)] = made[half:]
    made = times(hidden[block(1, 3)], project_s[:, QUERY]).astype(BF16)
    q2_s[block(0)] = made[:BLK]
    q2_s[block(3)] = made[BLK:]
    for copy in (k2_in, v2_in, q2_in):
        copy.wait()
    space_attention(
        4,
        lambda i: offset + i * BLK,
        lambda i: i * BLK,
        tables,
        (q2_s, 0, 0),
        (k2_s, 0, 0),
        (v2_s, 0, 0),
        *work,
    )
    middle_in.wait()
    update = times(mixed_s[...], output_s[...])
    state_ref[block(0)] = (edge_s[block(1)].astype(F32) + update[block(0)]).astype(BF16)
    state_ref[block(1, 3)] = (middle_s[...].astype(F32) + update[block(1, 3)]).astype(BF16)
    state_ref[block(3)] = (edge_s[block(2)].astype(F32) + update[block(3)]).astype(BF16)
    hidden_ref[...] = norm_rows(state_ref[...], time_gain_ref[...])


def time_kernel(
    frame_len,
    local_rows,
    devices,
    count_ref,
    index_ref,
    x_hbm,
    project_hbm,
    output_hbm,
    update_hbm,
    x_s,
    project_s,
    output_s,
    qkv_s,
    update_s,
    mixed_s,
    bias_s,
    scores_s,
    expon_s,
    in_sems,
    out_sems,
):
    groups, _, group, _ = x_s.shape
    rows = F * group
    piece = local_rows // devices
    *x_in, query_in, key_in, value_in, output_in = copies(
        in_sems,
        *[(x_hbm.at[:, g * group : (g + 1) * group], x_s.at[g]) for g in range(groups)],
        (project_hbm.at[:, QUERY], project_s.at[:, QUERY]),
        (project_hbm.at[:, KEY], project_s.at[:, KEY]),
        (project_hbm.at[:, VALUE], project_s.at[:, VALUE]),
        (output_hbm, output_s),
    )
    row = lax.broadcasted_iota(jnp.int32, (rows, rows), 0)
    col = lax.broadcasted_iota(jnp.int32, (rows, rows), 1)
    key = lax.broadcasted_iota(jnp.int32, (1, rows), 1)
    least = jnp.zeros((1, rows), jnp.int32)
    for g in range(F):
        least = jnp.where(lax.div(key, group) == g, frame_len - count_ref[g], least)
    same = lax.rem(row, group) == lax.rem(col, group)
    for g in range(groups):
        slot = lax.rem(key, group) + g * group
        place = lax.div(slot, piece) * local_rows + lax.rem(slot, piece) + index_ref[0] * piece
        living = jnp.where(place >= least, 1, 0)
        bias_s[g] = jnp.where(same & ((living == 1) | (row == col)), 0.0, MASKED).astype(F32)

    for copy in x_in:
        copy.wait()
    x = x_s[...].reshape(groups * rows, D)
    for copy, cols in ((query_in, QUERY), (key_in, KEY), (value_in, VALUE)):
        copy.wait()
        qkv_s[:, cols] = times(x, project_s[:, cols]).astype(BF16)
    output_in.wait()

    for g in range(groups):
        part = slice(g * rows, (g + 1) * rows)

        def columns(first):
            return lambda lanes: qkv_s[part, first + lanes.start : first + lanes.stop]

        def store(lanes, mixed):
            mixed_s[part, lanes] = mixed

        attention(columns(0), columns(D), columns(2 * D), store, bias_s.at[g], scores_s, expon_s)
    out = []
    for g in range(groups):
        part = slice(g * rows, (g + 1) * rows)
        update = times(mixed_s[part], output_s[...]).astype(BF16)
        update_s[g] = update.reshape(F, group, D)
        out += copies(
            out_sems.at[g : g + 1], (update_s.at[g], update_hbm.at[:, g * group : (g + 1) * group])
        )
    for copy in out:
        copy.wait()


def smem():
    return pl.BlockSpec(memory_space=pltpu.SMEM)


def vmem():
    return pl.BlockSpec(memory_space=pltpu.VMEM)


def hbm():
    return pl.BlockSpec(memory_space=pl.ANY)


def rows16(rows, cols):
    return jax.ShapeDtypeStruct((rows, cols), BF16)


def scratch(rows, cols):
    return pltpu.VMEM((rows, cols), BF16)


def work(mixed_rows, rows, keys, masks=()):
    return [
        scratch(mixed_rows, D),
        pltpu.VMEM((*masks, rows, keys), F32),
        pltpu.VMEM((H // 2, 2 * rows, keys), F32),
        pltpu.VMEM((H // 2, 2 * rows, keys), BF16),
    ]


def sems(count):
    return pltpu.SemaphoreType.DMA((count,))


def call(kernel, flops, exps, **rest):
    return pl.pallas_call(
        kernel,
        compiler_params=pltpu.CompilerParams(vmem_limit_bytes=VMEM_LIMIT),
        cost_estimate=pl.CostEstimate(
            flops=flops, bytes_accessed=16 * D * D, transcendentals=exps
        ),
        **rest,
    )


def on_device(
    frame_tokens,
    window_reach,
    valid_count,
    space_gain,
    space_project,
    space_output,
    time_gain,
    time_project,
    time_output,
):
    devices = lax.axis_size("strip")
    local_rows = frame_tokens.shape[0]
    total = local_rows * devices
    frame_len = total // F
    slots = local_rows // F
    groups = 2
    group = slots // groups
    if local_rows != 2 * CHUNK or frame_len % local_rows or local_rows % devices:
        raise ValueError("unsupported sizes")
    index = lax.axis_index("strip").reshape(1)

    up = [(i, i + 1) for i in range(devices - 1)]
    down = [(i + 1, i) for i in range(devices - 1)]
    before = lax.ppermute(frame_tokens[local_rows - CHUNK :], "strip", up)
    after = lax.ppermute(frame_tokens[:CHUNK], "strip", down)

    first, middle, second = call(
        functools.partial(middle_kernel, frame_len, total),
        2 * D * D * 10 * CHUNK,
        H * CHUNK * WIN,
        out_shape=(rows16(local_rows, 3 * D), rows16(CHUNK, D), rows16(CHUNK, 3 * D)),
        in_specs=[smem()] * 3 + [vmem()] + [hbm()] * 3,
        out_specs=(hbm(),) * 3,
        scratch_shapes=[
            scratch(local_rows, D),
            scratch(D, 3 * D),
            scratch(D, D),
            scratch(local_rows, 3 * D),
            scratch(CHUNK, D),
            scratch(CHUNK, 3 * D),
            *work(CHUNK, BLK, WIN),
            sems(5),
            sems(3),
        ],
    )(window_reach, valid_count, index, space_gain, frame_tokens, space_project, space_output)

    state, hidden = call(
        functools.partial(sides_kernel, frame_len, total),
        2 * D * D * 20 * CHUNK,
        4 * H * CHUNK * WIN,
        out_shape=(rows16(local_rows, D),) * 2,
        in_specs=[smem()] * 3 + [vmem()] * 2 + [hbm()] * 8,
        out_specs=(vmem(),) * 2,
        scratch_shapes=[
            scratch(local_rows, D),
            scratch(local_rows, D),
            scratch(CHUNK, D),
            scratch(D, 3 * D),
            scratch(D, D),
            scratch(local_rows, D),
            scratch(local_rows + 2 * CHUNK, D),
            scratch(local_rows + 2 * CHUNK, D),
            scratch(local_rows, D),
            scratch(local_rows + CHUNK, D),
            scratch(local_rows + CHUNK, D),
            *work(local_rows, BLK, WIN),
            sems(16),
        ],
    )(
        window_reach,
        valid_count,
        index,
        space_gain,
        time_gain,
        before,
        after,
        frame_tokens,
        first,
        middle,
        second,
        space_project,
        space_output,
    )

    def exchange(x):
        return lax.all_to_all(x, "strip", split_axis=0, concat_axis=0, tiled=True)

    gathered = exchange(hidden).reshape(F, slots, D)
    update = call(
        functools.partial(time_kernel, frame_len, local_rows, devices),
        2 * D * D * 10 * CHUNK,
        2 * H * CHUNK * CHUNK,
        out_shape=jax.ShapeDtypeStruct((F, slots, D), BF16),
        in_specs=[smem()] * 2 + [hbm()] * 3,
        out_specs=hbm(),
        scratch_shapes=[
            pltpu.VMEM((groups, F, group, D), BF16),
            scratch(D, 3 * D),
            scratch(D, D),
            scratch(local_rows, 3 * D),
            pltpu.VMEM((groups, F, group, D), BF16),
            *work(local_rows, F * group, F * group, (groups,)),
            sems(4 + groups),
            sems(groups),
        ],
    )(valid_count, index, gathered, time_project, time_output)
    returned = exchange(update.reshape(local_rows, D))
    return (state.astype(F32) + returned.astype(F32)).astype(BF16)


def solution(mesh):
    return jax.shard_map(
        on_device,
        mesh=mesh,
        in_specs=(
            P(("group", "strip"), None),
            P("group"),
            P("group"),
            P(),
            P(),
            P(),
            P(),
            P(),
            P(),
        ),
        out_specs=P(("group", "strip"), None),
        check_vma=False,
    )
```

```python
import functools

import jax
import jax.numpy as jnp
from jax import lax
from jax.experimental import pallas as pl
from jax.experimental.pallas import tpu as pltpu
from jax.sharding import PartitionSpec as P


F = 16
HALO = 128
H = 12
HD = 64
D = 768
BLK = HALO
WIN = 3 * BLK
PAIR = 2 * HD
CHUNK = 2 * BLK
MIB = 1 << 20
EPS = 1e-06
MASKED = -1e30

BF16 = jnp.bfloat16
F32 = jnp.float32


def norm_rows(values, gain):
    wide = values.astype(F32)
    meansq = jnp.mean(wide * wide, axis=-1, keepdims=True)
    return (wide * lax.rsqrt(meansq + EPS) * gain.reshape(1, D)).astype(BF16)


def pair_scores(q, k):
    lane = lax.broadcasted_iota(jnp.int32, (1, PAIR), 1)
    scale = HD ** (-0.5)
    left = jnp.where(lane < HD, scale, 0.0).astype(BF16)
    right = jnp.where(lane < HD, 0.0, scale).astype(BF16)
    both = jnp.concatenate([q * left, q * right], axis=0)
    return lax.dot_general(both, k, (((1,), (1,)), ((), ())), preferred_element_type=F32)


def pair_expon(scores, bias):
    rows, keys = bias.shape
    scores = scores.reshape(2, rows, keys) + bias[None]
    highest = jnp.max(scores, axis=-1, keepdims=True)
    return jnp.exp(scores - highest).reshape(2 * rows, keys).astype(BF16)


def pair_mixed(expon, v):
    rows = expon.shape[0] // 2
    lane = lax.broadcasted_iota(jnp.int32, (1, PAIR), 1)
    mixed = jnp.dot(
        expon, jnp.concatenate([v, jnp.ones_like(v)], axis=1), preferred_element_type=F32
    )
    mixed = (mixed[:, :PAIR] * (1.0 / mixed[:, PAIR:])).reshape(2, rows, PAIR)
    return jnp.where(lane < HD, mixed[0], mixed[1]).astype(BF16)


def lanes_of(pair):
    return slice(pair * PAIR, (pair + 1) * PAIR)


def attention(query, key, value, store, bias_ref, scores_s, expon_s):
    for pair in range(H // 2):
        scores_s[pair] = pair_scores(query(lanes_of(pair)), key(lanes_of(pair)))
    for pair in range(H // 2):
        expon_s[pair] = pair_expon(scores_s[pair], bias_ref[...])
    for pair in range(H // 2):
        store(lanes_of(pair), pair_mixed(expon_s[pair], value(lanes_of(pair))))


def window_bias(start, reach_ref, count_ref, frame_len, total):
    row = lax.broadcasted_iota(jnp.int32, (BLK, WIN), 0)
    col = lax.broadcasted_iota(jnp.int32, (BLK, WIN), 1)
    distance = col - BLK - row
    reach = reach_ref[lax.div(jnp.clip(start, 0, total - 1), frame_len)]
    least = jnp.zeros((1, WIN), jnp.int32)
    place = lax.broadcasted_iota(jnp.int32, (1, WIN), 1)
    for j in range(3):
        at = start + (j - 1) * BLK
        inside = (at >= 0) & (at < total)
        frame = lax.div(jnp.clip(at, 0, total - 1), frame_len)
        first = (frame + 1) * frame_len - count_ref[frame] - at
        first = jnp.where(inside, first, WIN) + j * BLK
        least = jnp.where(place >= j * BLK, first, least)
    living = (col >= least) | (distance == 0)
    return jnp.where((jnp.abs(distance) <= reach) & living, 0.0, MASKED).astype(F32)


def space_attention(blocks, start_of, window_of, tables, q, k, v, mixed_s, bias_s, scores_s, expon_s):
    def load(what, at, length):
        ref, row, column = what
        rows = pl.ds(pl.multiple_of(row + at, BLK), length)
        return lambda lanes: ref[rows, column + lanes.start : column + lanes.stop]

    def one_block(i, carry):
        bias_s[...] = window_bias(start_of(i), *tables)
        rows = pl.ds(pl.multiple_of(i * BLK, BLK), BLK)

        def store(lanes, mixed):
            mixed_s[rows, lanes] = mixed

        attention(
            load(q, i * BLK, BLK),
            load(k, window_of(i), WIN),
            load(v, window_of(i), WIN),
            store,
            bias_s,
            scores_s,
            expon_s,
        )
        return carry

    lax.fori_loop(0, blocks, one_block, 0)


def times(x, weight):
    return jnp.dot(x, weight, preferred_element_type=F32)


def copies(sems, *pairs):
    made = [pltpu.make_async_copy(a, b, sems.at[i]) for i, (a, b) in enumerate(pairs)]
    for copy in made:
        copy.start()
    return made


QUERY, KEY, VALUE = slice(0, D), slice(D, 2 * D), slice(2 * D, 3 * D)


def middle_kernel(
    frame_len,
    total,
    reach_ref,
    count_ref,
    index_ref,
    gain_ref,
    x_hbm,
    project_hbm,
    output_hbm,
    first_hbm,
    state_hbm,
    second_hbm,
    x_s,
    project_s,
    output_s,
    first_s,
    state_s,
    second_s,
    mixed_s,
    bias_s,
    scores_s,
    expon_s,
    in_sems,
    out_sems,
):
    rows = x_s.shape[0]
    offset = index_ref[0] * rows
    gain = gain_ref[...]
    inner = slice(BLK, rows - BLK)
    x_in, query_in, key_in, value_in, output_in = copies(
        in_sems,
        (x_hbm, x_s),
        (project_hbm.at[:, QUERY], project_s.at[:, QUERY]),
        (project_hbm.at[:, KEY], project_s.at[:, KEY]),
        (project_hbm.at[:, VALUE], project_s.at[:, VALUE]),
        (output_hbm, output_s),
    )
    x_in.wait()
    hidden = norm_rows(x_s[...], gain)
    for copy, cols in ((query_in, QUERY), (key_in, KEY), (value_in, VALUE)):
        copy.wait()
        first_s[:, cols] = times(hidden, project_s[:, cols]).astype(BF16)
    first_out = pltpu.make_async_copy(first_s, first_hbm, out_sems.at[0])
    first_out.start()
    tables = (reach_ref, count_ref, frame_len, total)
    space_attention(
        2,
        lambda i: offset + (i + 1) * BLK,
        lambda i: i * BLK,
        tables,
        (first_s, BLK, 0),
        (first_s, 0, D),
        (first_s, 0, 2 * D),
        mixed_s,
        bias_s,
        scores_s,
        expon_s,
    )
    output_in.wait()
    state_s[...] = (x_s[inner].astype(F32) + times(mixed_s[...], output_s[...])).astype(BF16)
    state_out = pltpu.make_async_copy(state_s, state_hbm, out_sems.at[1])
    state_out.start()
    hidden = norm_rows(state_s[...], gain)
    for cols in (QUERY, KEY, VALUE):
        second_s[:, cols] = times(hidden, project_s[:, cols]).astype(BF16)
    second_out = pltpu.make_async_copy(second_s, second_hbm, out_sems.at[2])
    second_out.start()
    first_out.wait()
    state_out.wait()
    second_out.wait()


def sides_kernel(
    frame_len,
    total,
    reach_ref,
    count_ref,
    index_ref,
    gain_ref,
    time_gain_ref,
    before_ref,
    after_ref,
    x_ref,
    first_ref,
    middle_ref,
    second_ref,
    project_ref,
    output_ref,
    state_ref,
    hidden_ref,
    edge_s,
    q_s,
    k_s,
    v_s,
    q2_s,
    k2_s,
    v2_s,
    mixed_s,
    bias_s,
    scores_s,
    expon_s,
    in_sems,
):
    rows = x_ref.shape[0]
    offset = index_ref[0] * rows
    gain = gain_ref[...]
    half = 2 * BLK

    def block(first, last=None):
        return slice(first * BLK, (first + 1 if last is None else last) * BLK)

    moved = copies(
        in_sems,
        (first_ref.at[:, KEY], k_s.at[block(2, 6)]),
        (first_ref.at[:, VALUE], v_s.at[block(2, 6)]),
        (first_ref.at[block(0), QUERY], q_s.at[block(1)]),
        (first_ref.at[block(3), QUERY], q_s.at[block(2)]),
    )
    moved2 = copies(
        in_sems.at[4:7],
        (second_ref.at[:, KEY], k2_s.at[block(2, 4)]),
        (second_ref.at[:, VALUE], v2_s.at[block(2, 4)]),
        (second_ref.at[:, QUERY], q2_s.at[block(1, 3)]),
    )
    tables = (reach_ref, count_ref, frame_len, total)
    work = (mixed_s, bias_s, scores_s, expon_s)
    halo = jnp.concatenate([before_ref[...], after_ref[...]], axis=0)
    hidden = norm_rows(halo, gain)
    for cols, ref in ((KEY, k_s), (VALUE, v_s)):
        made = times(hidden, project_ref[:, cols]).astype(BF16)
        ref[block(0, 2)] = made[:half]
        ref[block(6, 8)] = made[half:]
    made = times(hidden[block(1, 3)], project_ref[:, QUERY]).astype(BF16)
    q_s[block(0)] = made[:BLK]
    q_s[block(3)] = made[BLK:]
    for copy in moved:
        copy.wait()

    def skip(i):
        return jnp.where(i >= 2, half, 0)

    space_attention(
        4,
        lambda i: offset + (i - 1) * BLK + skip(i),
        lambda i: i * BLK + skip(i),
        tables,
        (q_s, 0, 0),
        (k_s, 0, 0),
        (v_s, 0, 0),
        *work,
    )
    update = times(mixed_s[...], output_ref[...])
    edge_s[block(0)] = (before_ref[block(1)].astype(F32) + update[block(0)]).astype(BF16)
    edge_s[block(1)] = (x_ref[block(0)].astype(F32) + update[block(1)]).astype(BF16)
    edge_s[block(2)] = (x_ref[block(3)].astype(F32) + update[block(2)]).astype(BF16)
    edge_s[block(3)] = (after_ref[block(0)].astype(F32) + update[block(3)]).astype(BF16)

    hidden = norm_rows(edge_s[...], gain)
    for cols, ref in ((KEY, k2_s), (VALUE, v2_s)):
        made = times(hidden, project_ref[:, cols]).astype(BF16)
        ref[block(0, 2)] = made[:half]
        ref[block(4, 6)] = made[half:]
    made = times(hidden[block(1, 3)], project_ref[:, QUERY]).astype(BF16)
    q2_s[block(0)] = made[:BLK]
    q2_s[block(3)] = made[BLK:]
    for copy in moved2:
        copy.wait()
    space_attention(
        4,
        lambda i: offset + i * BLK,
        lambda i: i * BLK,
        tables,
        (q2_s, 0, 0),
        (k2_s, 0, 0),
        (v2_s, 0, 0),
        *work,
    )
    update = times(mixed_s[...], output_ref[...])
    state_ref[block(0)] = (edge_s[block(1)].astype(F32) + update[block(0)]).astype(BF16)
    state_ref[block(1, 3)] = (middle_ref[...].astype(F32) + update[block(1, 3)]).astype(BF16)
    state_ref[block(3)] = (edge_s[block(2)].astype(F32) + update[block(3)]).astype(BF16)
    hidden_ref[...] = norm_rows(state_ref[...], time_gain_ref[...])


def time_kernel(
    frame_len,
    local_rows,
    devices,
    count_ref,
    index_ref,
    x_ref,
    project_ref,
    output_ref,
    update_ref,
    qkv_s,
    mixed_s,
    bias_s,
    scores_s,
    expon_s,
):
    groups = bias_s.shape[0]
    group = x_ref.shape[1] // groups
    rows = F * group
    piece = local_rows // devices
    row = lax.broadcasted_iota(jnp.int32, (rows, rows), 0)
    col = lax.broadcasted_iota(jnp.int32, (rows, rows), 1)
    key = lax.broadcasted_iota(jnp.int32, (1, rows), 1)
    least = jnp.zeros((1, rows), jnp.int32)
    for g in range(F):
        least = jnp.where(lax.div(key, group) == g, frame_len - count_ref[g], least)
    same = lax.rem(row, group) == lax.rem(col, group)
    for g in range(groups):
        slot = lax.rem(key, group) + g * group
        place = lax.div(slot, piece) * local_rows + lax.rem(slot, piece) + index_ref[0] * piece
        living = jnp.where(place >= least, 1, 0)
        bias_s[g] = jnp.where(same & ((living == 1) | (row == col)), 0.0, MASKED).astype(F32)

    x = jnp.concatenate(
        [x_ref[:, g * group : (g + 1) * group].reshape(rows, D) for g in range(groups)], axis=0
    )
    for cols in (QUERY, KEY, VALUE):
        qkv_s[:, cols] = times(x, project_ref[:, cols]).astype(BF16)

    for g in range(groups):
        part = slice(g * rows, (g + 1) * rows)

        def columns(first):
            return lambda lanes: qkv_s[part, first + lanes.start : first + lanes.stop]

        def store(lanes, mixed):
            mixed_s[part, lanes] = mixed

        attention(columns(0), columns(D), columns(2 * D), store, bias_s.at[g], scores_s, expon_s)
    update = times(mixed_s[...], output_ref[...]).astype(BF16)
    for g in range(groups):
        part = update[g * rows : (g + 1) * rows].reshape(F, group, D)
        update_ref[:, g * group : (g + 1) * group] = part


def smem():
    return pl.BlockSpec(memory_space=pltpu.SMEM)


def vmem():
    return pl.BlockSpec(memory_space=pltpu.VMEM)


def hbm():
    return pl.BlockSpec(memory_space=pl.ANY)


def rows16(rows, cols):
    return jax.ShapeDtypeStruct((rows, cols), BF16)


def scratch(rows, cols):
    return pltpu.VMEM((rows, cols), BF16)


def work(mixed_rows, rows, keys, masks=()):
    return [
        scratch(mixed_rows, D),
        pltpu.VMEM((*masks, rows, keys), F32),
        pltpu.VMEM((H // 2, 2 * rows, keys), F32),
        pltpu.VMEM((H // 2, 2 * rows, keys), BF16),
    ]


def sems(count):
    return pltpu.SemaphoreType.DMA((count,))


def call(kernel, flops, exps, limit, **rest):
    return pl.pallas_call(
        kernel,
        compiler_params=pltpu.CompilerParams(vmem_limit_bytes=limit),
        cost_estimate=pl.CostEstimate(
            flops=flops, bytes_accessed=16 * D * D, transcendentals=exps
        ),
        **rest,
    )


def on_device(
    frame_tokens,
    window_reach,
    valid_count,
    space_gain,
    space_project,
    space_output,
    time_gain,
    time_project,
    time_output,
):
    devices = lax.axis_size("strip")
    local_rows = frame_tokens.shape[0]
    total = local_rows * devices
    frame_len = total // F
    slots = local_rows // F
    groups = 2
    group = slots // groups
    if local_rows != 2 * CHUNK or frame_len % local_rows or local_rows % devices:
        raise ValueError("unsupported sizes")
    index = lax.axis_index("strip").reshape(1)

    up = [(i, i + 1) for i in range(devices - 1)]
    down = [(i + 1, i) for i in range(devices - 1)]
    before = lax.ppermute(frame_tokens[local_rows - CHUNK :], "strip", up)
    after = lax.ppermute(frame_tokens[:CHUNK], "strip", down)

    first, middle, second = call(
        functools.partial(middle_kernel, frame_len, total),
        2 * D * D * 10 * CHUNK,
        H * CHUNK * WIN,
        40 * MIB,
        out_shape=(rows16(local_rows, 3 * D), rows16(CHUNK, D), rows16(CHUNK, 3 * D)),
        in_specs=[smem()] * 3 + [vmem()] + [hbm()] * 3,
        out_specs=(hbm(),) * 3,
        scratch_shapes=[
            scratch(local_rows, D),
            scratch(D, 3 * D),
            scratch(D, D),
            scratch(local_rows, 3 * D),
            scratch(CHUNK, D),
            scratch(CHUNK, 3 * D),
            *work(CHUNK, BLK, WIN),
            sems(5),
            sems(3),
        ],
    )(
        window_reach,
        valid_count,
        index,
        space_gain,
        frame_tokens,
        pltpu.with_memory_space_constraint(space_project, pltpu.HBM),
        pltpu.with_memory_space_constraint(space_output, pltpu.HBM),
    )

    state, hidden = call(
        functools.partial(sides_kernel, frame_len, total),
        2 * D * D * 20 * CHUNK,
        4 * H * CHUNK * WIN,
        26 * MIB,
        out_shape=(rows16(local_rows, D),) * 2,
        in_specs=[smem()] * 3 + [vmem()] * 5 + [hbm()] + [vmem()] * 4,
        out_specs=(vmem(),) * 2,
        scratch_shapes=[
            scratch(local_rows, D),
            scratch(local_rows, D),
            scratch(local_rows + 2 * CHUNK, D),
            scratch(local_rows + 2 * CHUNK, D),
            scratch(local_rows, D),
            scratch(local_rows + CHUNK, D),
            scratch(local_rows + CHUNK, D),
            *work(local_rows, BLK, WIN),
            sems(7),
        ],
    )(
        window_reach,
        valid_count,
        index,
        space_gain,
        time_gain,
        before,
        after,
        frame_tokens,
        first,
        middle,
        second,
        space_project,
        space_output,
    )

    def exchange(x):
        return lax.all_to_all(x, "strip", split_axis=0, concat_axis=0, tiled=True)

    gathered = exchange(hidden).reshape(F, slots, D)
    update = call(
        functools.partial(time_kernel, frame_len, local_rows, devices),
        2 * D * D * 10 * CHUNK,
        2 * H * CHUNK * CHUNK,
        30 * MIB,
        out_shape=jax.ShapeDtypeStruct((F, slots, D), BF16),
        in_specs=[smem()] * 2 + [vmem()] * 3,
        out_specs=vmem(),
        scratch_shapes=[
            scratch(local_rows, 3 * D),
            *work(local_rows, F * group, F * group, (groups,)),
        ],
    )(valid_count, index, gathered, time_project, time_output)
    returned = exchange(update.reshape(local_rows, D))
    return (state.astype(F32) + returned.astype(F32)).astype(BF16)


def solution(mesh):
    return jax.shard_map(
        on_device,
        mesh=mesh,
        in_specs=(
            P(("group", "strip"), None),
            P("group"),
            P("group"),
            P(),
            P(),
            P(),
            P(),
            P(),
            P(),
        ),
        out_specs=P(("group", "strip"), None),
        check_vma=False,
    )
```

```python
import functools

import jax
import jax.numpy as jnp
from jax import lax
from jax.experimental import pallas as pl
from jax.experimental.pallas import tpu as pltpu
from jax.sharding import PartitionSpec as P


F = 16
HALO = 128
H = 12
HD = 64
D = 768
BLK = HALO
WIN = 3 * BLK
PAIR = 2 * HD
CHUNK = 2 * BLK
MIB = 1 << 20
EPS = 1e-06
MASKED = -1e30

BF16 = jnp.bfloat16
F32 = jnp.float32


def norm_rows(values, gain):
    wide = values.astype(F32)
    meansq = jnp.mean(wide * wide, axis=-1, keepdims=True)
    return (wide * lax.rsqrt(meansq + EPS) * gain.reshape(1, D)).astype(BF16)


def pair_scores(q, k):
    lane = lax.broadcasted_iota(jnp.int32, (1, PAIR), 1)
    scale = HD ** (-0.5)
    left = jnp.where(lane < HD, scale, 0.0).astype(BF16)
    right = jnp.where(lane < HD, 0.0, scale).astype(BF16)
    both = jnp.concatenate([q * left, q * right], axis=0)
    return lax.dot_general(both, k, (((1,), (1,)), ((), ())), preferred_element_type=F32)


def pair_expon(scores, bias):
    rows, keys = bias.shape
    scores = scores.reshape(2, rows, keys) + bias[None]
    highest = jnp.max(scores, axis=-1, keepdims=True)
    return jnp.exp(scores - highest).reshape(2 * rows, keys).astype(BF16)


def pair_mixed(expon, v):
    rows = expon.shape[0] // 2
    lane = lax.broadcasted_iota(jnp.int32, (1, PAIR), 1)
    mixed = jnp.dot(
        expon, jnp.concatenate([v, jnp.ones_like(v)], axis=1), preferred_element_type=F32
    )
    mixed = (mixed[:, :PAIR] * (1.0 / mixed[:, PAIR:])).reshape(2, rows, PAIR)
    return jnp.where(lane < HD, mixed[0], mixed[1]).astype(BF16)


def lanes_of(pair):
    return slice(pair * PAIR, (pair + 1) * PAIR)


def attention(query, key, value, store, bias_ref, scores_s, expon_s):
    for pair in range(H // 2):
        scores_s[pair] = pair_scores(query(lanes_of(pair)), key(lanes_of(pair)))
    for pair in range(H // 2):
        expon_s[pair] = pair_expon(scores_s[pair], bias_ref[...])
    for pair in range(H // 2):
        store(lanes_of(pair), pair_mixed(expon_s[pair], value(lanes_of(pair))))


def window_bias(start, reach_ref, count_ref, frame_len, total):
    row = lax.broadcasted_iota(jnp.int32, (BLK, WIN), 0)
    col = lax.broadcasted_iota(jnp.int32, (BLK, WIN), 1)
    distance = col - BLK - row
    reach = reach_ref[lax.div(jnp.clip(start, 0, total - 1), frame_len)]
    least = jnp.zeros((1, WIN), jnp.int32)
    place = lax.broadcasted_iota(jnp.int32, (1, WIN), 1)
    for j in range(3):
        at = start + (j - 1) * BLK
        inside = (at >= 0) & (at < total)
        frame = lax.div(jnp.clip(at, 0, total - 1), frame_len)
        first = (frame + 1) * frame_len - count_ref[frame] - at
        first = jnp.where(inside, first, WIN) + j * BLK
        least = jnp.where(place >= j * BLK, first, least)
    living = (col >= least) | (distance == 0)
    return jnp.where((jnp.abs(distance) <= reach) & living, 0.0, MASKED).astype(F32)


def space_attention(blocks, start_of, window_of, tables, q, k, v, mixed_s, bias_s, scores_s, expon_s):
    def load(what, at, length):
        ref, row, column = what
        rows = pl.ds(pl.multiple_of(row + at, BLK), length)
        return lambda lanes: ref[rows, column + lanes.start : column + lanes.stop]

    def one_block(i, carry):
        bias_s[...] = window_bias(start_of(i), *tables)
        rows = pl.ds(pl.multiple_of(i * BLK, BLK), BLK)

        def store(lanes, mixed):
            mixed_s[rows, lanes] = mixed

        attention(
            load(q, i * BLK, BLK),
            load(k, window_of(i), WIN),
            load(v, window_of(i), WIN),
            store,
            bias_s,
            scores_s,
            expon_s,
        )
        return carry

    lax.fori_loop(0, blocks, one_block, 0, unroll=True)


def times(x, weight):
    return jnp.dot(x, weight, preferred_element_type=F32)


def copies(sems, *pairs):
    made = [pltpu.make_async_copy(a, b, sems.at[i]) for i, (a, b) in enumerate(pairs)]
    for copy in made:
        copy.start()
    return made


QUERY, KEY, VALUE = slice(0, D), slice(D, 2 * D), slice(2 * D, 3 * D)


def middle_kernel(
    frame_len,
    total,
    reach_ref,
    count_ref,
    index_ref,
    gain_ref,
    x_ref,
    project_hbm,
    output_hbm,
    first_hbm,
    state_hbm,
    second_hbm,
    project_s,
    output_s,
    first_s,
    state_s,
    second_s,
    mixed_s,
    bias_s,
    scores_s,
    expon_s,
    in_sems,
    out_sems,
):
    rows = x_ref.shape[0]
    offset = index_ref[0] * rows
    gain = gain_ref[...]
    inner = slice(BLK, rows - BLK)
    query_in, key_in, value_in, output_in = copies(
        in_sems,
        (project_hbm.at[:, QUERY], project_s.at[:, QUERY]),
        (project_hbm.at[:, KEY], project_s.at[:, KEY]),
        (project_hbm.at[:, VALUE], project_s.at[:, VALUE]),
        (output_hbm, output_s),
    )
    hidden = norm_rows(x_ref[...], gain)
    for copy, cols in ((query_in, QUERY), (key_in, KEY), (value_in, VALUE)):
        copy.wait()
        first_s[:, cols] = times(hidden, project_s[:, cols]).astype(BF16)
    first_out = pltpu.make_async_copy(first_s, first_hbm, out_sems.at[0])
    first_out.start()
    tables = (reach_ref, count_ref, frame_len, total)
    space_attention(
        2,
        lambda i: offset + (i + 1) * BLK,
        lambda i: i * BLK,
        tables,
        (first_s, BLK, 0),
        (first_s, 0, D),
        (first_s, 0, 2 * D),
        mixed_s,
        bias_s,
        scores_s,
        expon_s,
    )
    output_in.wait()
    state_s[...] = (x_ref[inner].astype(F32) + times(mixed_s[...], output_s[...])).astype(BF16)
    state_out = pltpu.make_async_copy(state_s, state_hbm, out_sems.at[1])
    state_out.start()
    hidden = norm_rows(state_s[...], gain)
    for cols in (QUERY, KEY, VALUE):
        second_s[:, cols] = times(hidden, project_s[:, cols]).astype(BF16)
    second_out = pltpu.make_async_copy(second_s, second_hbm, out_sems.at[2])
    second_out.start()
    first_out.wait()
    state_out.wait()
    second_out.wait()


def sides_kernel(
    frame_len,
    total,
    reach_ref,
    count_ref,
    index_ref,
    gain_ref,
    time_gain_ref,
    before_ref,
    after_ref,
    x_ref,
    first_ref,
    middle_ref,
    second_ref,
    project_ref,
    output_ref,
    state_ref,
    hidden_ref,
    edge_s,
    q_s,
    k_s,
    v_s,
    q2_s,
    k2_s,
    v2_s,
    mixed_s,
    bias_s,
    scores_s,
    expon_s,
    in_sems,
):
    rows = x_ref.shape[0]
    offset = index_ref[0] * rows
    gain = gain_ref[...]
    half = 2 * BLK

    def block(first, last=None):
        return slice(first * BLK, (first + 1 if last is None else last) * BLK)

    moved = copies(
        in_sems,
        (first_ref.at[:, KEY], k_s.at[block(2, 6)]),
        (first_ref.at[:, VALUE], v_s.at[block(2, 6)]),
        (first_ref.at[block(0), QUERY], q_s.at[block(1)]),
        (first_ref.at[block(3), QUERY], q_s.at[block(2)]),
    )
    moved2 = copies(
        in_sems.at[4:7],
        (second_ref.at[:, KEY], k2_s.at[block(2, 4)]),
        (second_ref.at[:, VALUE], v2_s.at[block(2, 4)]),
        (second_ref.at[:, QUERY], q2_s.at[block(1, 3)]),
    )
    tables = (reach_ref, count_ref, frame_len, total)
    work = (mixed_s, bias_s, scores_s, expon_s)
    halo = jnp.concatenate([before_ref[...], after_ref[...]], axis=0)
    hidden = norm_rows(halo, gain)
    for cols, ref in ((KEY, k_s), (VALUE, v_s)):
        made = times(hidden, project_ref[:, cols]).astype(BF16)
        ref[block(0, 2)] = made[:half]
        ref[block(6, 8)] = made[half:]
    made = times(hidden[block(1, 3)], project_ref[:, QUERY]).astype(BF16)
    q_s[block(0)] = made[:BLK]
    q_s[block(3)] = made[BLK:]
    for copy in moved:
        copy.wait()

    def skip(i):
        return jnp.where(i >= 2, half, 0)

    space_attention(
        4,
        lambda i: offset + (i - 1) * BLK + skip(i),
        lambda i: i * BLK + skip(i),
        tables,
        (q_s, 0, 0),
        (k_s, 0, 0),
        (v_s, 0, 0),
        *work,
    )
    update = times(mixed_s[...], output_ref[...])
    edge_s[block(0)] = (before_ref[block(1)].astype(F32) + update[block(0)]).astype(BF16)
    edge_s[block(1)] = (x_ref[block(0)].astype(F32) + update[block(1)]).astype(BF16)
    edge_s[block(2)] = (x_ref[block(3)].astype(F32) + update[block(2)]).astype(BF16)
    edge_s[block(3)] = (after_ref[block(0)].astype(F32) + update[block(3)]).astype(BF16)

    hidden = norm_rows(edge_s[...], gain)
    for cols, ref in ((KEY, k2_s), (VALUE, v2_s)):
        made = times(hidden, project_ref[:, cols]).astype(BF16)
        ref[block(0, 2)] = made[:half]
        ref[block(4, 6)] = made[half:]
    made = times(hidden[block(1, 3)], project_ref[:, QUERY]).astype(BF16)
    q2_s[block(0)] = made[:BLK]
    q2_s[block(3)] = made[BLK:]
    for copy in moved2:
        copy.wait()
    space_attention(
        4,
        lambda i: offset + i * BLK,
        lambda i: i * BLK,
        tables,
        (q2_s, 0, 0),
        (k2_s, 0, 0),
        (v2_s, 0, 0),
        *work,
    )
    update = times(mixed_s[...], output_ref[...])
    state_ref[block(0)] = (edge_s[block(1)].astype(F32) + update[block(0)]).astype(BF16)
    state_ref[block(1, 3)] = (middle_ref[...].astype(F32) + update[block(1, 3)]).astype(BF16)
    state_ref[block(3)] = (edge_s[block(2)].astype(F32) + update[block(3)]).astype(BF16)
    hidden_ref[...] = norm_rows(state_ref[...], time_gain_ref[...])


def time_kernel(
    frame_len,
    local_rows,
    devices,
    count_ref,
    index_ref,
    x_ref,
    project_ref,
    output_ref,
    update_ref,
    qkv_s,
    mixed_s,
    bias_s,
    scores_s,
    expon_s,
):
    groups = bias_s.shape[0]
    group = x_ref.shape[1] // groups
    rows = F * group
    piece = local_rows // devices
    row = lax.broadcasted_iota(jnp.int32, (rows, rows), 0)
    col = lax.broadcasted_iota(jnp.int32, (rows, rows), 1)
    key = lax.broadcasted_iota(jnp.int32, (1, rows), 1)
    least = jnp.zeros((1, rows), jnp.int32)
    for g in range(F):
        least = jnp.where(lax.div(key, group) == g, frame_len - count_ref[g], least)
    same = lax.rem(row, group) == lax.rem(col, group)
    for g in range(groups):
        slot = lax.rem(key, group) + g * group
        place = lax.div(slot, piece) * local_rows + lax.rem(slot, piece) + index_ref[0] * piece
        living = jnp.where(place >= least, 1, 0)
        bias_s[g] = jnp.where(same & ((living == 1) | (row == col)), 0.0, MASKED).astype(F32)

    x = jnp.concatenate(
        [x_ref[:, g * group : (g + 1) * group].reshape(rows, D) for g in range(groups)], axis=0
    )
    for cols in (QUERY, KEY, VALUE):
        qkv_s[:, cols] = times(x, project_ref[:, cols]).astype(BF16)

    for g in range(groups):
        part = slice(g * rows, (g + 1) * rows)

        def columns(first):
            return lambda lanes: qkv_s[part, first + lanes.start : first + lanes.stop]

        def store(lanes, mixed):
            mixed_s[part, lanes] = mixed

        attention(columns(0), columns(D), columns(2 * D), store, bias_s.at[g], scores_s, expon_s)
    update = times(mixed_s[...], output_ref[...]).astype(BF16)
    for g in range(groups):
        part = update[g * rows : (g + 1) * rows].reshape(F, group, D)
        update_ref[:, g * group : (g + 1) * group] = part


def smem():
    return pl.BlockSpec(memory_space=pltpu.SMEM)


def vmem():
    return pl.BlockSpec(memory_space=pltpu.VMEM)


def hbm():
    return pl.BlockSpec(memory_space=pl.ANY)


def rows16(rows, cols):
    return jax.ShapeDtypeStruct((rows, cols), BF16)


def scratch(rows, cols):
    return pltpu.VMEM((rows, cols), BF16)


def work(mixed_rows, rows, keys, masks=()):
    return [
        scratch(mixed_rows, D),
        pltpu.VMEM((*masks, rows, keys), F32),
        pltpu.VMEM((H // 2, 2 * rows, keys), F32),
        pltpu.VMEM((H // 2, 2 * rows, keys), BF16),
    ]


def sems(count):
    return pltpu.SemaphoreType.DMA((count,))


def call(kernel, flops, exps, limit, **rest):
    return pl.pallas_call(
        kernel,
        compiler_params=pltpu.CompilerParams(vmem_limit_bytes=limit),
        cost_estimate=pl.CostEstimate(
            flops=flops, bytes_accessed=16 * D * D, transcendentals=exps
        ),
        **rest,
    )


def on_device(
    frame_tokens,
    window_reach,
    valid_count,
    space_gain,
    space_project,
    space_output,
    time_gain,
    time_project,
    time_output,
):
    devices = lax.axis_size("strip")
    local_rows = frame_tokens.shape[0]
    total = local_rows * devices
    frame_len = total // F
    slots = local_rows // F
    groups = 2
    group = slots // groups
    if local_rows != 2 * CHUNK or frame_len % local_rows or local_rows % devices:
        raise ValueError("unsupported sizes")
    index = lax.axis_index("strip").reshape(1)

    up = [(i, i + 1) for i in range(devices - 1)]
    down = [(i + 1, i) for i in range(devices - 1)]
    before = lax.ppermute(frame_tokens[local_rows - CHUNK :], "strip", up)
    after = lax.ppermute(frame_tokens[:CHUNK], "strip", down)

    first, middle, second, project, output = call(
        functools.partial(middle_kernel, frame_len, total),
        2 * D * D * 10 * CHUNK,
        H * CHUNK * WIN,
        40 * MIB,
        out_shape=(
            rows16(local_rows, 3 * D),
            rows16(CHUNK, D),
            rows16(CHUNK, 3 * D),
            rows16(D, 3 * D),
            rows16(D, D),
        ),
        in_specs=[smem()] * 3 + [vmem()] * 2 + [hbm()] * 2,
        out_specs=(hbm(),) * 3 + (vmem(),) * 2,
        scratch_shapes=[
            scratch(local_rows, 3 * D),
            scratch(CHUNK, D),
            scratch(CHUNK, 3 * D),
            *work(CHUNK, BLK, WIN),
            sems(4),
            sems(3),
        ],
    )(
        window_reach,
        valid_count,
        index,
        space_gain,
        frame_tokens,
        pltpu.with_memory_space_constraint(space_project, pltpu.HBM),
        pltpu.with_memory_space_constraint(space_output, pltpu.HBM),
    )

    state, hidden = call(
        functools.partial(sides_kernel, frame_len, total),
        2 * D * D * 20 * CHUNK,
        4 * H * CHUNK * WIN,
        26 * MIB,
        out_shape=(rows16(local_rows, D),) * 2,
        in_specs=[smem()] * 3 + [vmem()] * 5 + [hbm()] + [vmem()] * 4,
        out_specs=(vmem(),) * 2,
        scratch_shapes=[
            scratch(local_rows, D),
            scratch(local_rows, D),
            scratch(local_rows + 2 * CHUNK, D),
            scratch(local_rows + 2 * CHUNK, D),
            scratch(local_rows, D),
            scratch(local_rows + CHUNK, D),
            scratch(local_rows + CHUNK, D),
            *work(local_rows, BLK, WIN),
            sems(7),
        ],
    )(
        window_reach,
        valid_count,
        index,
        space_gain,
        time_gain,
        before,
        after,
        frame_tokens,
        first,
        middle,
        second,
        project,
        output,
    )

    def exchange(x):
        return lax.all_to_all(x, "strip", split_axis=0, concat_axis=0, tiled=True)

    gathered = exchange(hidden).reshape(F, slots, D)
    update = call(
        functools.partial(time_kernel, frame_len, local_rows, devices),
        2 * D * D * 10 * CHUNK,
        2 * H * CHUNK * CHUNK,
        30 * MIB,
        out_shape=jax.ShapeDtypeStruct((F, slots, D), BF16),
        in_specs=[smem()] * 2 + [vmem()] * 3,
        out_specs=vmem(),
        scratch_shapes=[
            scratch(local_rows, 3 * D),
            *work(local_rows, F * group, F * group, (groups,)),
        ],
    )(valid_count, index, gathered, time_project, time_output)
    returned = exchange(update.reshape(local_rows, D))
    return (state.astype(F32) + returned.astype(F32)).astype(BF16)


def solution(mesh):
    return jax.shard_map(
        on_device,
        mesh=mesh,
        in_specs=(
            P(("group", "strip"), None),
            P("group"),
            P("group"),
            P(),
            P(),
            P(),
            P(),
            P(),
            P(),
        ),
        out_specs=P(("group", "strip"), None),
        check_vma=False,
    )
```

```python
import functools

import jax
import jax.numpy as jnp
from jax import lax
from jax.experimental import pallas as pl
from jax.experimental.pallas import tpu as pltpu
from jax.sharding import PartitionSpec as P


F = 16
HALO = 128
H = 12
HD = 64
D = 768
BLK = HALO
WIN = 3 * BLK
PAIR = 2 * HD
CHUNK = 2 * BLK
MIB = 1 << 20
EPS = 1e-06
MASKED = -1e30

BF16 = jnp.bfloat16
F32 = jnp.float32


def norm_rows(values, gain):
    wide = values.astype(F32)
    meansq = jnp.mean(wide * wide, axis=-1, keepdims=True)
    return (wide * lax.rsqrt(meansq + EPS) * gain.reshape(1, D)).astype(BF16)


def pair_scores(q, k):
    lane = lax.broadcasted_iota(jnp.int32, (1, PAIR), 1)
    scale = HD ** (-0.5)
    left = jnp.where(lane < HD, scale, 0.0).astype(BF16)
    right = jnp.where(lane < HD, 0.0, scale).astype(BF16)
    both = jnp.concatenate([q * left, q * right], axis=0)
    return lax.dot_general(both, k, (((1,), (1,)), ((), ())), preferred_element_type=F32)


def pair_expon(scores, bias):
    rows, keys = bias.shape
    scores = scores.reshape(2, rows, keys) + bias[None]
    highest = jnp.max(scores, axis=-1, keepdims=True)
    return jnp.exp(scores - highest).reshape(2 * rows, keys).astype(BF16)


def pair_mixed(expon, v):
    rows = expon.shape[0] // 2
    lane = lax.broadcasted_iota(jnp.int32, (1, PAIR), 1)
    mixed = jnp.dot(
        expon, jnp.concatenate([v, jnp.ones_like(v)], axis=1), preferred_element_type=F32
    )
    mixed = (mixed[:, :PAIR] * (1.0 / mixed[:, PAIR:])).reshape(2, rows, PAIR)
    return jnp.where(lane < HD, mixed[0], mixed[1]).astype(BF16)


def lanes_of(pair):
    return slice(pair * PAIR, (pair + 1) * PAIR)


def attention(query, key, value, store, bias_ref, scores_s, expon_s):
    for pair in range(H // 2):
        scores_s[pair] = pair_scores(query(lanes_of(pair)), key(lanes_of(pair)))
    for pair in range(H // 2):
        expon_s[pair] = pair_expon(scores_s[pair], bias_ref[...])
    for pair in range(H // 2):
        store(lanes_of(pair), pair_mixed(expon_s[pair], value(lanes_of(pair))))


def window_bias(start, reach_ref, count_ref, frame_len, total):
    row = lax.broadcasted_iota(jnp.int32, (BLK, WIN), 0)
    col = lax.broadcasted_iota(jnp.int32, (BLK, WIN), 1)
    distance = col - BLK - row
    reach = reach_ref[lax.div(jnp.clip(start, 0, total - 1), frame_len)]
    least = jnp.zeros((1, WIN), jnp.int32)
    place = lax.broadcasted_iota(jnp.int32, (1, WIN), 1)
    for j in range(3):
        at = start + (j - 1) * BLK
        inside = (at >= 0) & (at < total)
        frame = lax.div(jnp.clip(at, 0, total - 1), frame_len)
        first = (frame + 1) * frame_len - count_ref[frame] - at
        first = jnp.where(inside, first, WIN) + j * BLK
        least = jnp.where(place >= j * BLK, first, least)
    living = (col >= least) | (distance == 0)
    return jnp.where((jnp.abs(distance) <= reach) & living, 0.0, MASKED).astype(F32)


def space_attention(blocks, start_of, window_of, tables, q, k, v, mixed_s, bias_s, scores_s, expon_s):
    def load(what, at, length):
        ref, row, column = what
        rows = pl.ds(pl.multiple_of(row + at, BLK), length)
        return lambda lanes: ref[rows, column + lanes.start : column + lanes.stop]

    def one_block(i, carry):
        bias_s[...] = window_bias(start_of(i), *tables)
        rows = pl.ds(pl.multiple_of(i * BLK, BLK), BLK)

        def store(lanes, mixed):
            mixed_s[rows, lanes] = mixed

        attention(
            load(q, i * BLK, BLK),
            load(k, window_of(i), WIN),
            load(v, window_of(i), WIN),
            store,
            bias_s,
            scores_s,
            expon_s,
        )
        return carry

    lax.fori_loop(0, blocks, one_block, 0, unroll=True)


def times(x, weight):
    return jnp.dot(x, weight, preferred_element_type=F32)


def copies(sems, *pairs):
    made = [pltpu.make_async_copy(a, b, sems.at[i]) for i, (a, b) in enumerate(pairs)]
    for copy in made:
        copy.start()
    return made


QUERY, KEY, VALUE = slice(0, D), slice(D, 2 * D), slice(2 * D, 3 * D)


def middle_kernel(
    frame_len,
    total,
    reach_ref,
    count_ref,
    index_ref,
    gain_ref,
    x_ref,
    project_hbm,
    output_hbm,
    first_hbm,
    state_hbm,
    second_hbm,
    project_s,
    output_s,
    first_s,
    state_s,
    second_s,
    mixed_s,
    bias_s,
    scores_s,
    expon_s,
    in_sems,
    out_sems,
):
    rows = x_ref.shape[0]
    offset = index_ref[0] * rows
    gain = gain_ref[...]
    inner = slice(BLK, rows - BLK)
    query_in, key_in, value_in, output_in = copies(
        in_sems,
        (project_hbm.at[:, QUERY], project_s.at[:, QUERY]),
        (project_hbm.at[:, KEY], project_s.at[:, KEY]),
        (project_hbm.at[:, VALUE], project_s.at[:, VALUE]),
        (output_hbm, output_s),
    )
    hidden = norm_rows(x_ref[...], gain)
    for copy, cols in ((query_in, QUERY), (key_in, KEY), (value_in, VALUE)):
        copy.wait()
        first_s[:, cols] = times(hidden, project_s[:, cols]).astype(BF16)
    first_out = pltpu.make_async_copy(first_s, first_hbm, out_sems.at[0])
    first_out.start()
    tables = (reach_ref, count_ref, frame_len, total)
    space_attention(
        2,
        lambda i: offset + (i + 1) * BLK,
        lambda i: i * BLK,
        tables,
        (first_s, BLK, 0),
        (first_s, 0, D),
        (first_s, 0, 2 * D),
        mixed_s,
        bias_s,
        scores_s,
        expon_s,
    )
    output_in.wait()
    state_s[...] = (x_ref[inner].astype(F32) + times(mixed_s[...], output_s[...])).astype(BF16)
    state_out = pltpu.make_async_copy(state_s, state_hbm, out_sems.at[1])
    state_out.start()
    hidden = norm_rows(state_s[...], gain)
    for cols in (QUERY, KEY, VALUE):
        second_s[:, cols] = times(hidden, project_s[:, cols]).astype(BF16)
    second_out = pltpu.make_async_copy(second_s, second_hbm, out_sems.at[2])
    second_out.start()
    first_out.wait()
    state_out.wait()
    second_out.wait()


def sides_kernel(
    frame_len,
    total,
    reach_ref,
    count_ref,
    index_ref,
    gain_ref,
    time_gain_ref,
    near_ref,
    far_ref,
    x_ref,
    first_ref,
    middle_ref,
    second_ref,
    project_ref,
    output_ref,
    state_ref,
    hidden_ref,
    halo_s,
    edge_s,
    q_s,
    k_s,
    v_s,
    q2_s,
    k2_s,
    v2_s,
    mixed_s,
    bias_s,
    scores_s,
    expon_s,
    in_sems,
):
    rows = x_ref.shape[0]
    offset = index_ref[0] * rows
    gain = gain_ref[...]
    half = 2 * BLK

    def block(first, last=None):
        return slice(first * BLK, (first + 1 if last is None else last) * BLK)

    moved = copies(
        in_sems,
        (first_ref.at[:, KEY], k_s.at[block(2, 6)]),
        (first_ref.at[:, VALUE], v_s.at[block(2, 6)]),
        (first_ref.at[block(0), QUERY], q_s.at[block(1)]),
        (first_ref.at[block(3), QUERY], q_s.at[block(2)]),
    )
    moved2 = copies(
        in_sems.at[4:7],
        (second_ref.at[:, KEY], k2_s.at[block(2, 4)]),
        (second_ref.at[:, VALUE], v2_s.at[block(2, 4)]),
        (second_ref.at[:, QUERY], q2_s.at[block(1, 3)]),
    )
    tables = (reach_ref, count_ref, frame_len, total)
    work = (mixed_s, bias_s, scores_s, expon_s)
    odd = lax.rem(index_ref[0], 2)

    @pl.when(odd == 1)
    def _():
        halo_s[:half] = near_ref[...]
        halo_s[half:] = far_ref[...]

    @pl.when(odd == 0)
    def _():
        halo_s[:half] = far_ref[...]
        halo_s[half:] = near_ref[...]

    hidden = norm_rows(halo_s[...], gain)
    for cols, ref in ((KEY, k_s), (VALUE, v_s)):
        made = times(hidden, project_ref[:, cols]).astype(BF16)
        ref[block(0, 2)] = made[:half]
        ref[block(6, 8)] = made[half:]
    made = times(hidden[block(1, 3)], project_ref[:, QUERY]).astype(BF16)
    q_s[block(0)] = made[:BLK]
    q_s[block(3)] = made[BLK:]
    for copy in moved:
        copy.wait()

    def skip(i):
        return jnp.where(i >= 2, half, 0)

    space_attention(
        4,
        lambda i: offset + (i - 1) * BLK + skip(i),
        lambda i: i * BLK + skip(i),
        tables,
        (q_s, 0, 0),
        (k_s, 0, 0),
        (v_s, 0, 0),
        *work,
    )
    update = times(mixed_s[...], output_ref[...])
    edge_s[block(0)] = (halo_s[block(1)].astype(F32) + update[block(0)]).astype(BF16)
    edge_s[block(1)] = (x_ref[block(0)].astype(F32) + update[block(1)]).astype(BF16)
    edge_s[block(2)] = (x_ref[block(3)].astype(F32) + update[block(2)]).astype(BF16)
    edge_s[block(3)] = (halo_s[block(2)].astype(F32) + update[block(3)]).astype(BF16)

    hidden = norm_rows(edge_s[...], gain)
    for cols, ref in ((KEY, k2_s), (VALUE, v2_s)):
        made = times(hidden, project_ref[:, cols]).astype(BF16)
        ref[block(0, 2)] = made[:half]
        ref[block(4, 6)] = made[half:]
    made = times(hidden[block(1, 3)], project_ref[:, QUERY]).astype(BF16)
    q2_s[block(0)] = made[:BLK]
    q2_s[block(3)] = made[BLK:]
    for copy in moved2:
        copy.wait()
    space_attention(
        4,
        lambda i: offset + i * BLK,
        lambda i: i * BLK,
        tables,
        (q2_s, 0, 0),
        (k2_s, 0, 0),
        (v2_s, 0, 0),
        *work,
    )
    update = times(mixed_s[...], output_ref[...])
    state_ref[block(0)] = (edge_s[block(1)].astype(F32) + update[block(0)]).astype(BF16)
    state_ref[block(1, 3)] = (middle_ref[...].astype(F32) + update[block(1, 3)]).astype(BF16)
    state_ref[block(3)] = (edge_s[block(2)].astype(F32) + update[block(3)]).astype(BF16)
    hidden_ref[...] = norm_rows(state_ref[...], time_gain_ref[...])


def time_kernel(
    frame_len,
    local_rows,
    devices,
    count_ref,
    index_ref,
    x_ref,
    project_ref,
    output_ref,
    update_ref,
    qkv_s,
    mixed_s,
    bias_s,
    scores_s,
    expon_s,
):
    groups = bias_s.shape[0]
    group = x_ref.shape[1] // groups
    rows = F * group
    piece = local_rows // devices
    row = lax.broadcasted_iota(jnp.int32, (rows, rows), 0)
    col = lax.broadcasted_iota(jnp.int32, (rows, rows), 1)
    key = lax.broadcasted_iota(jnp.int32, (1, rows), 1)
    least = jnp.zeros((1, rows), jnp.int32)
    for g in range(F):
        least = jnp.where(lax.div(key, group) == g, frame_len - count_ref[g], least)
    same = lax.rem(row, group) == lax.rem(col, group)
    for g in range(groups):
        slot = lax.rem(key, group) + g * group
        place = lax.div(slot, piece) * local_rows + lax.rem(slot, piece) + index_ref[0] * piece
        living = jnp.where(place >= least, 1, 0)
        bias_s[g] = jnp.where(same & ((living == 1) | (row == col)), 0.0, MASKED).astype(F32)

    x = jnp.concatenate(
        [x_ref[:, g * group : (g + 1) * group].reshape(rows, D) for g in range(groups)], axis=0
    )
    for cols in (QUERY, KEY, VALUE):
        qkv_s[:, cols] = times(x, project_ref[:, cols]).astype(BF16)

    for g in range(groups):
        part = slice(g * rows, (g + 1) * rows)

        def columns(first):
            return lambda lanes: qkv_s[part, first + lanes.start : first + lanes.stop]

        def store(lanes, mixed):
            mixed_s[part, lanes] = mixed

        attention(columns(0), columns(D), columns(2 * D), store, bias_s.at[g], scores_s, expon_s)
    update = times(mixed_s[...], output_ref[...]).astype(BF16)
    for g in range(groups):
        part = update[g * rows : (g + 1) * rows].reshape(F, group, D)
        update_ref[:, g * group : (g + 1) * group] = part


def smem():
    return pl.BlockSpec(memory_space=pltpu.SMEM)


def vmem():
    return pl.BlockSpec(memory_space=pltpu.VMEM)


def hbm():
    return pl.BlockSpec(memory_space=pl.ANY)


def rows16(rows, cols):
    return jax.ShapeDtypeStruct((rows, cols), BF16)


def scratch(rows, cols):
    return pltpu.VMEM((rows, cols), BF16)


def work(mixed_rows, rows, keys, masks=()):
    return [
        scratch(mixed_rows, D),
        pltpu.VMEM((*masks, rows, keys), F32),
        pltpu.VMEM((H // 2, 2 * rows, keys), F32),
        pltpu.VMEM((H // 2, 2 * rows, keys), BF16),
    ]


def sems(count):
    return pltpu.SemaphoreType.DMA((count,))


def call(kernel, flops, exps, limit, **rest):
    return pl.pallas_call(
        kernel,
        compiler_params=pltpu.CompilerParams(vmem_limit_bytes=limit),
        cost_estimate=pl.CostEstimate(
            flops=flops, bytes_accessed=16 * D * D, transcendentals=exps
        ),
        **rest,
    )


def on_device(
    frame_tokens,
    window_reach,
    valid_count,
    space_gain,
    space_project,
    space_output,
    time_gain,
    time_project,
    time_output,
):
    devices = lax.axis_size("strip")
    local_rows = frame_tokens.shape[0]
    total = local_rows * devices
    frame_len = total // F
    slots = local_rows // F
    groups = 2
    group = slots // groups
    if devices % 2 or local_rows != 2 * CHUNK or frame_len % local_rows or local_rows % devices:
        raise ValueError("unsupported sizes")
    index = lax.axis_index("strip").reshape(1)

    partners = [(i, i ^ 1) for i in range(devices)]
    others = [(i, i + 1 if i % 2 else i - 1) for i in range(1, devices - 1)]
    odd = lax.rem(lax.axis_index("strip"), 2)
    last = local_rows - CHUNK
    near = lax.ppermute(
        lax.dynamic_slice_in_dim(frame_tokens, (1 - odd) * last, CHUNK), "strip", partners
    )
    far = lax.ppermute(lax.dynamic_slice_in_dim(frame_tokens, odd * last, CHUNK), "strip", others)

    first, middle, second, project, output = call(
        functools.partial(middle_kernel, frame_len, total),
        2 * D * D * 10 * CHUNK,
        H * CHUNK * WIN,
        40 * MIB,
        out_shape=(
            rows16(local_rows, 3 * D),
            rows16(CHUNK, D),
            rows16(CHUNK, 3 * D),
            rows16(D, 3 * D),
            rows16(D, D),
        ),
        in_specs=[smem()] * 3 + [vmem()] * 2 + [hbm()] * 2,
        out_specs=(hbm(),) * 3 + (vmem(),) * 2,
        scratch_shapes=[
            scratch(local_rows, 3 * D),
            scratch(CHUNK, D),
            scratch(CHUNK, 3 * D),
            *work(CHUNK, BLK, WIN),
            sems(4),
            sems(3),
        ],
    )(
        window_reach,
        valid_count,
        index,
        space_gain,
        frame_tokens,
        pltpu.with_memory_space_constraint(space_project, pltpu.HBM),
        pltpu.with_memory_space_constraint(space_output, pltpu.HBM),
    )

    state, hidden = call(
        functools.partial(sides_kernel, frame_len, total),
        2 * D * D * 20 * CHUNK,
        4 * H * CHUNK * WIN,
        26 * MIB,
        out_shape=(rows16(local_rows, D),) * 2,
        in_specs=[smem()] * 3 + [vmem()] * 5 + [hbm()] + [vmem()] * 4,
        out_specs=(vmem(),) * 2,
        scratch_shapes=[
            scratch(local_rows, D),
            scratch(local_rows, D),
            scratch(local_rows, D),
            scratch(local_rows + 2 * CHUNK, D),
            scratch(local_rows + 2 * CHUNK, D),
            scratch(local_rows, D),
            scratch(local_rows + CHUNK, D),
            scratch(local_rows + CHUNK, D),
            *work(local_rows, BLK, WIN),
            sems(7),
        ],
    )(
        window_reach,
        valid_count,
        index,
        space_gain,
        time_gain,
        near,
        far,
        frame_tokens,
        first,
        middle,
        second,
        project,
        output,
    )

    def exchange(x):
        return lax.all_to_all(x, "strip", split_axis=0, concat_axis=0, tiled=True)

    gathered = exchange(hidden).reshape(F, slots, D)
    update = call(
        functools.partial(time_kernel, frame_len, local_rows, devices),
        2 * D * D * 10 * CHUNK,
        2 * H * CHUNK * CHUNK,
        30 * MIB,
        out_shape=jax.ShapeDtypeStruct((F, slots, D), BF16),
        in_specs=[smem()] * 2 + [vmem()] * 3,
        out_specs=vmem(),
        scratch_shapes=[
            scratch(local_rows, 3 * D),
            *work(local_rows, F * group, F * group, (groups,)),
        ],
    )(valid_count, index, gathered, time_project, time_output)
    returned = exchange(update.reshape(local_rows, D))
    return (state.astype(F32) + returned.astype(F32)).astype(BF16)


def solution(mesh):
    return jax.shard_map(
        on_device,
        mesh=mesh,
        in_specs=(
            P(("group", "strip"), None),
            P("group"),
            P("group"),
            P(),
            P(),
            P(),
            P(),
            P(),
            P(),
        ),
        out_specs=P(("group", "strip"), None),
        check_vma=False,
    )
```

```python
import functools

import jax
import jax.numpy as jnp
from jax import lax
from jax.experimental import pallas as pl
from jax.experimental.pallas import tpu as pltpu
from jax.sharding import PartitionSpec as P


F = 16
HALO = 128
H = 12
HD = 64
D = 768
BLK = HALO
WIN = 3 * BLK
PAIR = 2 * HD
CHUNK = 2 * BLK
MIB = 1 << 20
EPS = 1e-06
MASKED = -1e30

BF16 = jnp.bfloat16
F32 = jnp.float32


def norm_rows(values, gain):
    wide = values.astype(F32)
    meansq = jnp.mean(wide * wide, axis=-1, keepdims=True)
    return (wide * lax.rsqrt(meansq + EPS) * gain.reshape(1, D)).astype(BF16)


def pair_scores(q, k):
    lane = lax.broadcasted_iota(jnp.int32, (1, PAIR), 1)
    scale = HD ** (-0.5)
    left = jnp.where(lane < HD, scale, 0.0).astype(BF16)
    right = jnp.where(lane < HD, 0.0, scale).astype(BF16)
    both = jnp.concatenate([q * left, q * right], axis=0)
    return lax.dot_general(both, k, (((1,), (1,)), ((), ())), preferred_element_type=F32)


def pair_expon(scores, bias):
    rows, keys = bias.shape
    scores = scores.reshape(2, rows, keys) + bias[None]
    highest = jnp.max(scores, axis=-1, keepdims=True)
    return jnp.exp(scores - highest).reshape(2 * rows, keys).astype(BF16)


def pair_mixed(expon, v):
    rows = expon.shape[0] // 2
    lane = lax.broadcasted_iota(jnp.int32, (1, PAIR), 1)
    mixed = jnp.dot(
        expon, jnp.concatenate([v, jnp.ones_like(v)], axis=1), preferred_element_type=F32
    )
    mixed = (mixed[:, :PAIR] * (1.0 / mixed[:, PAIR:])).reshape(2, rows, PAIR)
    return jnp.where(lane < HD, mixed[0], mixed[1]).astype(BF16)


def lanes_of(pair):
    return slice(pair * PAIR, (pair + 1) * PAIR)


def attention(query, key, value, store, bias_ref, scores_s, expon_s):
    for pair in range(H // 2):
        scores_s[pair] = pair_scores(query(lanes_of(pair)), key(lanes_of(pair)))
    for pair in range(H // 2):
        expon_s[pair] = pair_expon(scores_s[pair], bias_ref[...])
    for pair in range(H // 2):
        store(lanes_of(pair), pair_mixed(expon_s[pair], value(lanes_of(pair))))


def window_bias(start, reach_ref, count_ref, frame_len, total):
    row = lax.broadcasted_iota(jnp.int32, (BLK, WIN), 0)
    col = lax.broadcasted_iota(jnp.int32, (BLK, WIN), 1)
    distance = col - BLK - row
    reach = reach_ref[lax.div(jnp.clip(start, 0, total - 1), frame_len)]
    least = jnp.zeros((1, WIN), jnp.int32)
    place = lax.broadcasted_iota(jnp.int32, (1, WIN), 1)
    for j in range(3):
        at = start + (j - 1) * BLK
        inside = (at >= 0) & (at < total)
        frame = lax.div(jnp.clip(at, 0, total - 1), frame_len)
        first = (frame + 1) * frame_len - count_ref[frame] - at
        first = jnp.where(inside, first, WIN) + j * BLK
        least = jnp.where(place >= j * BLK, first, least)
    living = (col >= least) | (distance == 0)
    return jnp.where((jnp.abs(distance) <= reach) & living, 0.0, MASKED).astype(F32)


def space_attention(blocks, start_of, window_of, tables, q, k, v, mixed_s, bias_s, scores_s, expon_s):
    def load(what, at, length):
        ref, row, column = what
        rows = pl.ds(pl.multiple_of(row + at, BLK), length)
        return lambda lanes: ref[rows, column + lanes.start : column + lanes.stop]

    def one_block(i, carry):
        bias_s[...] = window_bias(start_of(i), *tables)
        rows = pl.ds(pl.multiple_of(i * BLK, BLK), BLK)

        def store(lanes, mixed):
            mixed_s[rows, lanes] = mixed

        attention(
            load(q, i * BLK, BLK),
            load(k, window_of(i), WIN),
            load(v, window_of(i), WIN),
            store,
            bias_s,
            scores_s,
            expon_s,
        )
        return carry

    lax.fori_loop(0, blocks, one_block, 0, unroll=True)


def times(x, weight):
    return jnp.dot(x, weight, preferred_element_type=F32)


def copies(sems, *pairs):
    made = [pltpu.make_async_copy(a, b, sems.at[i]) for i, (a, b) in enumerate(pairs)]
    for copy in made:
        copy.start()
    return made


QUERY, KEY, VALUE = slice(0, D), slice(D, 2 * D), slice(2 * D, 3 * D)


def middle_kernel(
    frame_len,
    total,
    reach_ref,
    count_ref,
    index_ref,
    gain_ref,
    x_ref,
    project_hbm,
    output_hbm,
    first_s,
    state_s,
    second_s,
    project_s,
    output_s,
    mixed_s,
    bias_s,
    scores_s,
    expon_s,
    in_sems,
):
    rows = x_ref.shape[0]
    offset = index_ref[0] * rows
    gain = gain_ref[...]
    inner = slice(BLK, rows - BLK)
    query_in, key_in, value_in, output_in = copies(
        in_sems,
        (project_hbm.at[:, QUERY], project_s.at[:, QUERY]),
        (project_hbm.at[:, KEY], project_s.at[:, KEY]),
        (project_hbm.at[:, VALUE], project_s.at[:, VALUE]),
        (output_hbm, output_s),
    )
    hidden = norm_rows(x_ref[...], gain)
    for copy, cols in ((query_in, QUERY), (key_in, KEY), (value_in, VALUE)):
        copy.wait()
        first_s[:, cols] = times(hidden, project_s[:, cols]).astype(BF16)
    tables = (reach_ref, count_ref, frame_len, total)
    space_attention(
        2,
        lambda i: offset + (i + 1) * BLK,
        lambda i: i * BLK,
        tables,
        (first_s, BLK, 0),
        (first_s, 0, D),
        (first_s, 0, 2 * D),
        mixed_s,
        bias_s,
        scores_s,
        expon_s,
    )
    output_in.wait()
    state_s[...] = (x_ref[inner].astype(F32) + times(mixed_s[...], output_s[...])).astype(BF16)
    hidden = norm_rows(state_s[...], gain)
    for cols in (QUERY, KEY, VALUE):
        second_s[:, cols] = times(hidden, project_s[:, cols]).astype(BF16)


def sides_kernel(
    frame_len,
    total,
    reach_ref,
    count_ref,
    index_ref,
    gain_ref,
    time_gain_ref,
    near_ref,
    far_ref,
    x_ref,
    first_ref,
    middle_ref,
    second_ref,
    project_ref,
    output_ref,
    state_ref,
    hidden_ref,
    halo_s,
    edge_s,
    q_s,
    k_s,
    v_s,
    q2_s,
    k2_s,
    v2_s,
    mixed_s,
    bias_s,
    scores_s,
    expon_s,
    in_sems,
):
    rows = x_ref.shape[0]
    offset = index_ref[0] * rows
    gain = gain_ref[...]
    half = 2 * BLK

    def block(first, last=None):
        return slice(first * BLK, (first + 1 if last is None else last) * BLK)

    moved = copies(
        in_sems,
        (first_ref.at[:, KEY], k_s.at[block(2, 6)]),
        (first_ref.at[:, VALUE], v_s.at[block(2, 6)]),
        (first_ref.at[block(0), QUERY], q_s.at[block(1)]),
        (first_ref.at[block(3), QUERY], q_s.at[block(2)]),
    )
    moved2 = copies(
        in_sems.at[4:7],
        (second_ref.at[:, KEY], k2_s.at[block(2, 4)]),
        (second_ref.at[:, VALUE], v2_s.at[block(2, 4)]),
        (second_ref.at[:, QUERY], q2_s.at[block(1, 3)]),
    )
    tables = (reach_ref, count_ref, frame_len, total)
    work = (mixed_s, bias_s, scores_s, expon_s)
    odd = lax.rem(index_ref[0], 2)

    @pl.when(odd == 1)
    def _():
        halo_s[:half] = near_ref[...]
        halo_s[half:] = far_ref[...]

    @pl.when(odd == 0)
    def _():
        halo_s[:half] = far_ref[...]
        halo_s[half:] = near_ref[...]

    hidden = norm_rows(halo_s[...], gain)
    for cols, ref in ((KEY, k_s), (VALUE, v_s)):
        made = times(hidden, project_ref[:, cols]).astype(BF16)
        ref[block(0, 2)] = made[:half]
        ref[block(6, 8)] = made[half:]
    made = times(hidden[block(1, 3)], project_ref[:, QUERY]).astype(BF16)
    q_s[block(0)] = made[:BLK]
    q_s[block(3)] = made[BLK:]
    for copy in moved:
        copy.wait()

    def skip(i):
        return jnp.where(i >= 2, half, 0)

    space_attention(
        4,
        lambda i: offset + (i - 1) * BLK + skip(i),
        lambda i: i * BLK + skip(i),
        tables,
        (q_s, 0, 0),
        (k_s, 0, 0),
        (v_s, 0, 0),
        *work,
    )
    update = times(mixed_s[...], output_ref[...])
    edge_s[block(0)] = (halo_s[block(1)].astype(F32) + update[block(0)]).astype(BF16)
    edge_s[block(1)] = (x_ref[block(0)].astype(F32) + update[block(1)]).astype(BF16)
    edge_s[block(2)] = (x_ref[block(3)].astype(F32) + update[block(2)]).astype(BF16)
    edge_s[block(3)] = (halo_s[block(2)].astype(F32) + update[block(3)]).astype(BF16)

    hidden = norm_rows(edge_s[...], gain)
    for cols, ref in ((KEY, k2_s), (VALUE, v2_s)):
        made = times(hidden, project_ref[:, cols]).astype(BF16)
        ref[block(0, 2)] = made[:half]
        ref[block(4, 6)] = made[half:]
    made = times(hidden[block(1, 3)], project_ref[:, QUERY]).astype(BF16)
    q2_s[block(0)] = made[:BLK]
    q2_s[block(3)] = made[BLK:]
    for copy in moved2:
        copy.wait()
    space_attention(
        4,
        lambda i: offset + i * BLK,
        lambda i: i * BLK,
        tables,
        (q2_s, 0, 0),
        (k2_s, 0, 0),
        (v2_s, 0, 0),
        *work,
    )
    update = times(mixed_s[...], output_ref[...])
    state_ref[block(0)] = (edge_s[block(1)].astype(F32) + update[block(0)]).astype(BF16)
    state_ref[block(1, 3)] = (middle_ref[...].astype(F32) + update[block(1, 3)]).astype(BF16)
    state_ref[block(3)] = (edge_s[block(2)].astype(F32) + update[block(3)]).astype(BF16)
    hidden_ref[...] = norm_rows(state_ref[...], time_gain_ref[...])


def time_kernel(
    frame_len,
    local_rows,
    devices,
    count_ref,
    index_ref,
    x_ref,
    project_ref,
    output_ref,
    update_ref,
    qkv_s,
    mixed_s,
    bias_s,
    scores_s,
    expon_s,
):
    groups = bias_s.shape[0]
    group = x_ref.shape[1] // groups
    rows = F * group
    piece = local_rows // devices
    row = lax.broadcasted_iota(jnp.int32, (rows, rows), 0)
    col = lax.broadcasted_iota(jnp.int32, (rows, rows), 1)
    key = lax.broadcasted_iota(jnp.int32, (1, rows), 1)
    least = jnp.zeros((1, rows), jnp.int32)
    for g in range(F):
        least = jnp.where(lax.div(key, group) == g, frame_len - count_ref[g], least)
    same = lax.rem(row, group) == lax.rem(col, group)
    for g in range(groups):
        slot = lax.rem(key, group) + g * group
        place = lax.div(slot, piece) * local_rows + lax.rem(slot, piece) + index_ref[0] * piece
        living = jnp.where(place >= least, 1, 0)
        bias_s[g] = jnp.where(same & ((living == 1) | (row == col)), 0.0, MASKED).astype(F32)

    x = jnp.concatenate(
        [x_ref[:, g * group : (g + 1) * group].reshape(rows, D) for g in range(groups)], axis=0
    )
    for cols in (QUERY, KEY, VALUE):
        qkv_s[:, cols] = times(x, project_ref[:, cols]).astype(BF16)

    for g in range(groups):
        part = slice(g * rows, (g + 1) * rows)

        def columns(first):
            return lambda lanes: qkv_s[part, first + lanes.start : first + lanes.stop]

        def store(lanes, mixed):
            mixed_s[part, lanes] = mixed

        attention(columns(0), columns(D), columns(2 * D), store, bias_s.at[g], scores_s, expon_s)
    update = times(mixed_s[...], output_ref[...]).astype(BF16)
    for g in range(groups):
        part = update[g * rows : (g + 1) * rows].reshape(F, group, D)
        update_ref[:, g * group : (g + 1) * group] = part


def smem():
    return pl.BlockSpec(memory_space=pltpu.SMEM)


def vmem():
    return pl.BlockSpec(memory_space=pltpu.VMEM)


def hbm():
    return pl.BlockSpec(memory_space=pl.ANY)


def rows16(rows, cols):
    return jax.ShapeDtypeStruct((rows, cols), BF16)


def scratch(rows, cols):
    return pltpu.VMEM((rows, cols), BF16)


def work(mixed_rows, rows, keys, masks=()):
    return [
        scratch(mixed_rows, D),
        pltpu.VMEM((*masks, rows, keys), F32),
        pltpu.VMEM((H // 2, 2 * rows, keys), F32),
        pltpu.VMEM((H // 2, 2 * rows, keys), BF16),
    ]


def sems(count):
    return pltpu.SemaphoreType.DMA((count,))


def call(kernel, flops, exps, limit, **rest):
    return pl.pallas_call(
        kernel,
        compiler_params=pltpu.CompilerParams(vmem_limit_bytes=limit),
        cost_estimate=pl.CostEstimate(
            flops=flops, bytes_accessed=16 * D * D, transcendentals=exps
        ),
        **rest,
    )


def on_device(
    frame_tokens,
    window_reach,
    valid_count,
    space_gain,
    space_project,
    space_output,
    time_gain,
    time_project,
    time_output,
):
    devices = lax.axis_size("strip")
    local_rows = frame_tokens.shape[0]
    total = local_rows * devices
    frame_len = total // F
    slots = local_rows // F
    groups = 2
    group = slots // groups
    if devices % 2 or local_rows != 2 * CHUNK or frame_len % local_rows or local_rows % devices:
        raise ValueError("unsupported sizes")
    index = lax.axis_index("strip").reshape(1)

    partners = [(i, i ^ 1) for i in range(devices)]
    others = [(i, i + 1 if i % 2 else i - 1) for i in range(1, devices - 1)]
    odd = lax.rem(lax.axis_index("strip"), 2)
    last = local_rows - CHUNK
    near = lax.ppermute(
        lax.dynamic_slice_in_dim(frame_tokens, (1 - odd) * last, CHUNK), "strip", partners
    )
    far = lax.ppermute(lax.dynamic_slice_in_dim(frame_tokens, odd * last, CHUNK), "strip", others)

    first, middle, second, project, output = call(
        functools.partial(middle_kernel, frame_len, total),
        2 * D * D * 10 * CHUNK,
        H * CHUNK * WIN,
        40 * MIB,
        out_shape=(
            rows16(local_rows, 3 * D),
            rows16(CHUNK, D),
            rows16(CHUNK, 3 * D),
            rows16(D, 3 * D),
            rows16(D, D),
        ),
        in_specs=[smem()] * 3 + [vmem()] * 2 + [hbm()] * 2,
        out_specs=(vmem(),) * 5,
        scratch_shapes=[
            *work(CHUNK, BLK, WIN),
            sems(4),
        ],
    )(
        window_reach,
        valid_count,
        index,
        space_gain,
        frame_tokens,
        pltpu.with_memory_space_constraint(space_project, pltpu.HBM),
        pltpu.with_memory_space_constraint(space_output, pltpu.HBM),
    )

    state, hidden = call(
        functools.partial(sides_kernel, frame_len, total),
        2 * D * D * 20 * CHUNK,
        4 * H * CHUNK * WIN,
        26 * MIB,
        out_shape=(rows16(local_rows, D),) * 2,
        in_specs=[smem()] * 3 + [vmem()] * 5 + [hbm()] + [vmem()] * 4,
        out_specs=(vmem(),) * 2,
        scratch_shapes=[
            scratch(local_rows, D),
            scratch(local_rows, D),
            scratch(local_rows, D),
            scratch(local_rows + 2 * CHUNK, D),
            scratch(local_rows + 2 * CHUNK, D),
            scratch(local_rows, D),
            scratch(local_rows + CHUNK, D),
            scratch(local_rows + CHUNK, D),
            *work(local_rows, BLK, WIN),
            sems(7),
        ],
    )(
        window_reach,
        valid_count,
        index,
        space_gain,
        time_gain,
        near,
        far,
        frame_tokens,
        first,
        middle,
        second,
        project,
        output,
    )

    def exchange(x):
        return lax.all_to_all(x, "strip", split_axis=0, concat_axis=0, tiled=True)

    gathered = exchange(hidden).reshape(F, slots, D)
    update = call(
        functools.partial(time_kernel, frame_len, local_rows, devices),
        2 * D * D * 10 * CHUNK,
        2 * H * CHUNK * CHUNK,
        30 * MIB,
        out_shape=jax.ShapeDtypeStruct((F, slots, D), BF16),
        in_specs=[smem()] * 2 + [vmem()] * 3,
        out_specs=vmem(),
        scratch_shapes=[
            scratch(local_rows, 3 * D),
            *work(local_rows, F * group, F * group, (groups,)),
        ],
    )(valid_count, index, gathered, time_project, time_output)
    returned = exchange(update.reshape(local_rows, D))
    return (state.astype(F32) + returned.astype(F32)).astype(BF16)


def solution(mesh):
    return jax.shard_map(
        on_device,
        mesh=mesh,
        in_specs=(
            P(("group", "strip"), None),
            P("group"),
            P("group"),
            P(),
            P(),
            P(),
            P(),
            P(),
            P(),
        ),
        out_specs=P(("group", "strip"), None),
        check_vma=False,
    )
```
